32 devices in a mesh: dp: 16 (over z, y, core), tensor: 2 (over x).
Axes of the slice: x: 2, y: 2, z: 4, core: 2. Of those that a mesh axis runs over, the one named last changes fastest.
Arguments:
- h_in: bfloat16 [16, 2, 512, 768], P('dp', None, 'tensor'), may hold values from -6 to 6
- g_in: bfloat16 [16, 2, 512, 768], P('dp', None, 'tensor'), may hold values from -6 to 6
- mem_in: bfloat16 [16, 2, 384, 768], P('dp', None, 'tensor'), may hold values from -6 to 6
- d_h_out: bfloat16 [16, 2, 512, 768], P('dp', None, 'tensor'), may hold values from -6 to 6
- d_g_out: bfloat16 [16, 2, 512, 768], P('dp', None, 'tensor'), may hold values from -6 to 6
- w_query: bfloat16 [768, 768], P(None, 'tensor'), may hold values from -0.21875 to 0.21875
- w_key: bfloat16 [768, 768], P(None, 'tensor'), may hold values from -0.21875 to 0.21875
- w_value: bfloat16 [768, 768], P(None, 'tensor'), may hold values from -0.21875 to 0.21875
- w_out: bfloat16 [768, 768], P('tensor'), may hold values from -0.875 to 0.875
- content_bias: float32 [12, 64], P('tensor'), may hold values from -3 to 3
- seg_bias: float32 [12, 64], P('tensor'), may hold values from -3 to 3
- seg_embed: float32 [2, 12, 64], P(None, 'tensor'), may hold values from -6 to 6
- rel_table: float32 [12, 32], P('tensor'), may hold values from -48 to 48
- norm1_gain: float32 [768], replicated, may hold values from 0.5 to 1.5
- norm1_bias: float32 [768], replicated, may hold values from -1.2 to 1.2
- w_in: bfloat16 [768, 3072], P(None, 'tensor'), may hold values from -0.21875 to 0.21875
- b_in: float32 [3072], P('tensor'), may hold values from -1.8 to 1.8
- w_ffo: bfloat16 [3072, 768], P('tensor'), may hold values from -0.109375 to 0.109375
- b_ffo: float32 [768], replicated, may hold values from -1.2 to 1.2
- norm2_gain: float32 [768], replicated, may hold values from 0.5 to 1.5
- norm2_bias: float32 [768], replicated, may hold values from -1.2 to 1.2
- bucket_len: int32 [16, 2], P('dp'), may hold values from 64 to 512, as said below
- doc_len: int32 [16, 2, 8], P('dp'), may hold values from 0 to 512, as said below
- seg_ids: int32 [16, 2, 512], P('dp'), may hold values from 0 to 1
- mem_seg: int32 [16, 2, 384], P('dp'), may hold values from 0 to 1
- perm_rank: int32 [16, 2, 512], P('dp'), may hold values from 0 to 63
Outputs:
- h_out: bfloat16 [16, 2, 512, 768], P('dp', None, 'tensor')
- g_out: bfloat16 [16, 2, 512, 768], P('dp', None, 'tensor')
- d_h_in: bfloat16 [16, 2, 512, 768], P('dp', None, 'tensor')
- d_g_in: bfloat16 [16, 2, 512, 768], P('dp', None, 'tensor')
- d_mem_in: bfloat16 [16, 2, 384, 768], P('dp', None, 'tensor')
- d_w_query: float32 [768, 768], P(None, 'tensor')
- d_w_key: float32 [768, 768], P(None, 'tensor')
- d_w_value: float32 [768, 768], P(None, 'tensor')
- d_w_out: float32 [768, 768], P('tensor')
- d_content_bias: float32 [12, 64], P('tensor')
- d_seg_bias: float32 [12, 64], P('tensor')
- d_seg_embed: float32 [2, 12, 64], P(None, 'tensor')
- d_rel_table: float32 [12, 32], P('tensor')
- d_norm1_gain: float32 [768], replicated
- d_norm1_bias: float32 [768], replicated
- d_w_in: float32 [768, 3072], P(None, 'tensor')
- d_b_in: float32 [3072], P('tensor')
- d_w_ffo: float32 [3072, 768], P('tensor')
- d_b_ffo: float32 [768], replicated
- d_norm2_gain: float32 [768], replicated
- d_norm2_bias: float32 [768], replicated
The draws below stay inside these ranges and needn't reach their ends.
Inputs may be any that keep to these rules, and one draw needn't show every extreme that they name: `bucket_len`: every entry is 512, 256, 128 or 64; counting slots group by group, the first slot of all is 512 and the second 512 // 8. `doc_len`: for a slot whose bucket_len is b, entry k is 0 when k * b >= 512, else between b // 2 and b; entry 0 equals b.
All inputs are finite; a program needn't handle non-finite values.
Results may differ from the reference program's by a relative error of at most 0.03.
Values may be sent and summed in bfloat16 or wider, within the bound.
No kernel may reach another device: no remote copies, remote signals or barrier semaphores. Data moves between devices by JAX's collectives and lax.ppermute only.
A program may use at most 320 MiB of HBM per device.

```python
import jax
import jax.numpy as jnp
from jax import lax

D = 768
HEADS = 12
HDIM = 64
FF = 3072
NREL = 32
SLOT = 512
MEM = 384
MAXDOC = 8
SEQ_DEV = 2
GROUPS = 16


def layout_draw(key):
    kind_key, length_key = jax.random.split(jax.random.fold_in(key, 17))
    kind_draw = jax.random.randint(kind_key, (GROUPS * SEQ_DEV,), 0, 8)
    bucket = jnp.where(kind_draw == 0, SLOT, jnp.where(kind_draw <= 2, SLOT // 2, jnp.where(kind_draw <= 5, SLOT // 4, SLOT // 8)))
    bucket = bucket.at[0].set(SLOT).at[1].set(SLOT // 8).astype(jnp.int32)
    bucket = bucket.reshape(GROUPS, SEQ_DEV)
    doc_index = jnp.arange(MAXDOC, dtype=jnp.int32)
    shortfall = jax.random.randint(length_key, (GROUPS, SEQ_DEV, MAXDOC), 0, SLOT // 2 + 1)
    shortfall = shortfall % (bucket[:, :, None] // 2 + 1)
    lengths = jnp.where(doc_index == 0, bucket[:, :, None], bucket[:, :, None] - shortfall)
    lengths = jnp.where(doc_index * bucket[:, :, None] < SLOT, lengths, 0)
    return (bucket, lengths.astype(jnp.int32))


def draw_bucket_len(key, part):
    return layout_draw(key)[0]


def draw_doc_len(key, part):
    return layout_draw(key)[1]


def plant(result, rng, smallest, high):
    index_at = [jax.random.randint(jax.random.fold_in(rng, axis), (), 0, length) for axis, length in enumerate(result.shape)]
    main_axis = result.shape.index(max(result.shape))
    neighbour = index_at[:main_axis] + [(index_at[main_axis] + 1) % result.shape[main_axis]] + index_at[main_axis + 1:]
    return result.at[tuple(index_at)].set(smallest).at[tuple(neighbour)].set(high)


def level_of(own_key, shape, shards, low, largest):
    def one(dim, blocks):
        draws = jax.random.uniform(jax.random.fold_in(jax.random.fold_in(own_key, 6), dim), (blocks,), jnp.float32, low / len(shards), largest / len(shards))
        return jnp.repeat(jnp.exp(draws), shape[dim] // blocks).reshape((-1,) + (1,) * (len(shape) - dim - 1))

    loudness = one(*shards[0])
    for cut in shards[1:]:
        loudness = loudness * one(*cut)
    return loudness


def bell_draw(own_key, extent, scale, limit, pieces=(), kind=jnp.bfloat16):
    array = scale * jax.random.normal(own_key, extent, jnp.float32)
    if pieces:
        array = array * level_of(own_key, extent, pieces, -0.22, 0.18)
    return jnp.clip(array, -limit, limit).astype(kind)


def setup_inputs(seed: int = 0) -> dict:
    streams_of = jax.random.split(jax.random.key(seed), 27)
    h_in = bell_draw(streams_of[0], (GROUPS, SEQ_DEV, SLOT, D), 1.0, 6.0, ((0, 16), (2, 2)))
    g_in = bell_draw(streams_of[1], (GROUPS, SEQ_DEV, SLOT, D), 1.0, 6.0, ((0, 16), (2, 2)))
    mem_in = bell_draw(streams_of[2], (GROUPS, SEQ_DEV, MEM, D), 1.0, 6.0, ((0, 16), (2, 2)))
    d_h_out = bell_draw(streams_of[3], (GROUPS, SEQ_DEV, SLOT, D), 1.0, 6.0, ((0, 16), (2, 2)))
    d_g_out = bell_draw(streams_of[4], (GROUPS, SEQ_DEV, SLOT, D), 1.0, 6.0, ((0, 16), (2, 2)))
    w_query = bell_draw(streams_of[5], (D, HEADS * HDIM), D ** -0.5, 0.21875, ((1, 2),))
    w_key = bell_draw(streams_of[6], (D, HEADS * HDIM), D ** -0.5, 0.21875, ((1, 2),))
    w_value = bell_draw(streams_of[7], (D, HEADS * HDIM), D ** -0.5, 0.21875, ((1, 2),))
    w_out = bell_draw(streams_of[8], (HEADS * HDIM, D), (D // 16) ** -0.5, 0.875, ((0, 2),))
    content_bias = bell_draw(streams_of[9], (HEADS, HDIM), 0.5, 3.0, ((0, 2),), jnp.float32)
    seg_bias = bell_draw(streams_of[10], (HEADS, HDIM), 0.5, 3.0, ((0, 2),), jnp.float32)
    seg_embed = bell_draw(streams_of[11], (2, HEADS, HDIM), 1.0, 6.0, ((1, 2),), jnp.float32)
    rel_table = bell_draw(streams_of[12], (HEADS, NREL), 8.0, 48.0, ((0, 2),), jnp.float32)
    norm1_gain = jnp.clip(1.0 + 0.1 * jax.random.normal(streams_of[13], (D,), jnp.float32), 0.5, 1.5)
    norm1_bias = bell_draw(streams_of[14], (D,), 0.2, 1.2, (), jnp.float32)
    w_in = bell_draw(streams_of[15], (D, FF), D ** -0.5, 0.21875, ((1, 2),))
    b_in = bell_draw(streams_of[16], (FF,), 0.3, 1.8, ((0, 2),), jnp.float32)
    w_ffo = bell_draw(streams_of[17], (FF, D), FF ** -0.5, 0.109375, ((0, 2),))
    b_ffo = bell_draw(streams_of[18], (D,), 0.2, 1.2, (), jnp.float32)
    norm2_gain = jnp.clip(1.0 + 0.1 * jax.random.normal(streams_of[19], (D,), jnp.float32), 0.5, 1.5)
    norm2_bias = bell_draw(streams_of[20], (D,), 0.2, 1.2, (), jnp.float32)
    bucket_len = draw_bucket_len(jax.random.fold_in(streams_of[26], 71), 0)
    doc_len = draw_doc_len(jax.random.fold_in(streams_of[26], 71), 0)
    seg_ids = plant(jax.random.randint(streams_of[23], (GROUPS, SEQ_DEV, SLOT), 0, 2), jax.random.fold_in(streams_of[23], 1), 0, 1).astype(jnp.int32)
    mem_seg = plant(jax.random.randint(streams_of[24], (GROUPS, SEQ_DEV, MEM), 0, 2), jax.random.fold_in(streams_of[24], 1), 0, 1).astype(jnp.int32)
    perm_rank = plant(jax.random.randint(streams_of[25], (GROUPS, SEQ_DEV, SLOT), 0, 64), jax.random.fold_in(streams_of[25], 1), 0, 63).astype(jnp.int32)
    return dict(h_in=h_in, g_in=g_in, mem_in=mem_in, d_h_out=d_h_out, d_g_out=d_g_out, w_query=w_query, w_key=w_key, w_value=w_value, w_out=w_out, content_bias=content_bias, seg_bias=seg_bias, seg_embed=seg_embed, rel_table=rel_table, norm1_gain=norm1_gain, norm1_bias=norm1_bias, w_in=w_in, b_in=b_in, w_ffo=w_ffo, b_ffo=b_ffo, norm2_gain=norm2_gain, norm2_bias=norm2_bias, bucket_len=bucket_len, doc_len=doc_len, seg_ids=seg_ids, mem_seg=mem_seg, perm_rank=perm_rank)


@jax.custom_vjp
def low(v):
    return lax.optimization_barrier(v.astype(jnp.bfloat16)).astype(jnp.float32)

@jax.custom_vjp
def low_back(v):
    return v

def low_keep(v):
    return (low(v), None)

def low_pass(kept, grad):
    return (grad,)

def back_keep(v):
    return (v, None)

def back_low(kept, grad):
    return (low(grad),)
low.defvjp(low_keep, low_pass)
low_back.defvjp(back_keep, back_low)
epsilon = 1e-05
masked_score = -1e+30
target_floor = 48
distance_steps = (1, 2, 3, 4, 5, 6, 7, 8, 12, 16, 24, 32, 64, 128, 256)
highest = lax.Precision.HIGHEST

def rounded(value):
    return low_back(low(value))

def bucket_of(distance):
    magnitude = jnp.abs(distance)
    counted = jnp.zeros(distance.shape, jnp.int32)
    for threshold in distance_steps:
        counted = counted + (magnitude >= threshold).astype(jnp.int32)
    return counted + NREL // 2 * (distance > 0).astype(jnp.int32)

def slot_masks(bucket, doc_len, perm_rank, seg_ids, mem_seg):
    slot_rows = perm_rank.shape[0]
    mem_rows = mem_seg.shape[0]
    positions = jnp.arange(slot_rows, dtype=jnp.int32)
    document = positions // bucket
    within = positions - document * bucket
    doc_index = jnp.arange(doc_len.shape[0], dtype=jnp.int32)
    doc_length = lax.optimization_barrier(jnp.sum(jnp.where(document[:, None] == doc_index[None, :], doc_len[None, :], 0), axis=1, dtype=jnp.int32))
    present = within < doc_length
    factor_order = jnp.where(within < 2, 0, jnp.maximum(perm_rank - target_floor, 0))
    same_doc = (document[:, None] == document[None, :]) & present[None, :]
    itself = positions[:, None] == positions[None, :]
    content_see = same_doc & (factor_order[None, :] <= factor_order[:, None]) | itself
    query_see = same_doc & jnp.logical_not(itself) & ((factor_order[None, :] < factor_order[:, None]) | (factor_order[None, :] == 0))
    memory_see = jnp.broadcast_to(bucket == slot_rows, (slot_rows, mem_rows))
    see_content = jnp.concatenate([memory_see, content_see], axis=1)
    see_query = jnp.concatenate([memory_see, query_see], axis=1)
    key_place = jnp.concatenate([jnp.arange(mem_rows, dtype=jnp.int32) - mem_rows, positions])
    buckets = bucket_of(positions[:, None] - key_place[None, :])
    same_seg = seg_ids[:, None] == jnp.concatenate([mem_seg, seg_ids])[None, :]
    return (see_content, see_query, buckets, same_seg)

def layer_norm(values_in, norm_gain, norm_bias):
    centred = values_in - lax.optimization_barrier(jnp.mean(values_in, axis=-1, keepdims=True))
    spread = lax.optimization_barrier(jnp.mean(centred * centred, axis=-1, keepdims=True))
    return centred * lax.rsqrt(spread + epsilon) * norm_gain + norm_bias

def attend(queries, key_rows, value_rows, visible, buckets, same_seg, content_bias, seg_bias, seg_embed, rel_table):
    scores = jnp.einsum('ihd,jhd->hij', queries, key_rows, precision=highest)
    scores = scores + jnp.einsum('hd,jhd->hj', content_bias, key_rows, precision=highest)[:, None, :]
    shifted = jnp.einsum('ihd,chd->chi', queries + seg_bias[None], seg_embed, precision=highest)
    scores = scores + jnp.where(same_seg[None], shifted[1][:, :, None], shifted[0][:, :, None])
    scores = scores + rel_table[:, buckets]
    scores = low_back(scores * HDIM ** (-0.5))
    scores = jnp.where(visible[None], scores, masked_score)
    weights = jax.nn.softmax(scores, axis=-1)
    attended = jnp.einsum('hij,jhd->ihd', low(weights), value_rows, precision=highest)
    return rounded(attended.reshape(attended.shape[0], -1))

def forward_slot(params, content, stream, memory, mask_set):
    w_query, w_key, w_value, w_out, content_bias, seg_bias, seg_embed, rel_table, norm1_gain, norm1_bias, w_in, b_in, w_ffo, b_ffo, norm2_gain, norm2_bias = params
    see_content, see_query, buckets, same_seg = mask_set

    def to_heads(values_in):
        return values_in.reshape(values_in.shape[0], HEADS, HDIM)
    key_input = jnp.concatenate([memory, content], axis=0)
    key_rows = to_heads(rounded(jnp.dot(key_input, w_key, precision=highest)))
    value_rows = to_heads(rounded(jnp.dot(key_input, w_value, precision=highest)))
    results = []
    for stream_rows, visible in ((content, see_content), (stream, see_query)):
        queries = to_heads(rounded(jnp.dot(stream_rows, w_query, precision=highest)))
        attended = attend(queries, key_rows, value_rows, visible, buckets, same_seg, content_bias, seg_bias, seg_embed, rel_table)
        normed = layer_norm(stream_rows + low_back(jnp.dot(attended, w_out, precision=highest)), norm1_gain, norm1_bias)
        hidden = low_back(jnp.dot(low(normed), w_in, precision=highest) + b_in)
        active = low(jax.nn.gelu(hidden, approximate=True))
        second = normed + low_back(jnp.dot(active, w_ffo, precision=highest) + b_ffo)
        results.append(layer_norm(second, norm2_gain, norm2_bias))
    return (results[0], results[1])

def reference(h_in, g_in, mem_in, d_h_out, d_g_out, w_query, w_key, w_value, w_out, content_bias, seg_bias, seg_embed, rel_table, norm1_gain, norm1_bias, w_in, b_in, w_ffo, b_ffo, norm2_gain, norm2_bias, bucket_len, doc_len, seg_ids, mem_seg, perm_rank):
    params = tuple((weight.astype(jnp.float32) for weight in (w_query, w_key, w_value, w_out, content_bias, seg_bias, seg_embed, rel_table, norm1_gain, norm1_bias, w_in, b_in, w_ffo, b_ffo, norm2_gain, norm2_bias)))

    def flatten(source):
        return source.reshape((-1,) + source.shape[2:])
    per_slot_in = tuple((flatten(source) for source in (h_in, g_in, mem_in, d_h_out, d_g_out, bucket_len, doc_len, seg_ids, mem_seg, perm_rank)))

    def one_slot(totals, slot_items):
        content, stream, memory, cot_content, cot_stream, bucket, lengths, segments, mem_segments, rank_slot = slot_items
        mask_set = slot_masks(bucket, lengths, rank_slot, segments, mem_segments)

        def forward(weights_in, content_in, stream_in, memory_in):
            return forward_slot(weights_in, content_in, stream_in, memory_in, mask_set)
        outputs, pullback = jax.vjp(forward, params, content.astype(jnp.float32), stream.astype(jnp.float32), memory.astype(jnp.float32))
        gradients = pullback((cot_content.astype(jnp.float32), cot_stream.astype(jnp.float32)))
        totals = jax.tree.map(jnp.add, totals, gradients[0])
        return (totals, (outputs[0].astype(jnp.bfloat16), outputs[1].astype(jnp.bfloat16), gradients[1].astype(jnp.bfloat16), gradients[2].astype(jnp.bfloat16), gradients[3].astype(jnp.bfloat16)))
    zero_grads = tuple((jnp.zeros_like(weight) for weight in params))
    totals, per_slot = lax.scan(one_slot, zero_grads, per_slot_in)
    shaped = tuple((member.reshape((GROUPS, SEQ_DEV) + member.shape[1:]) for member in per_slot))
    return (shaped[0], shaped[1], shaped[2], shaped[3], shaped[4], totals[0], totals[1], totals[2], totals[3], totals[4], totals[5], totals[6], totals[7], totals[8], totals[9], totals[10], totals[11], totals[12], totals[13], totals[14], totals[15])
```

```python
import jax
import jax.numpy as jnp
from jax import lax
from jax.experimental import pallas as pl
from jax.experimental.pallas import tpu as pltpu
from jax.sharding import PartitionSpec as P

HDIM = 64
NREL = 32
epsilon = 1e-05
masked_score = -1e30
target_floor = 48
distance_steps = (1, 2, 3, 4, 5, 6, 7, 8, 12, 16, 24, 32, 64, 128, 256)
highest = lax.Precision.HIGHEST
f32 = jnp.float32
bf16 = jnp.bfloat16
LANES = 128
ORDERS = 16
SCALE = HDIM ** (-0.5)


def bucket_of(distance):
    magnitude = jnp.abs(distance)
    counted = jnp.zeros(distance.shape, jnp.int32)
    for threshold in distance_steps:
        counted = counted + (magnitude >= threshold).astype(jnp.int32)
    return counted + NREL // 2 * (distance > 0).astype(jnp.int32)


def diagonal_buckets(half, rows, mem_rows):
    pieces = []
    for width, off in (
        (rows, 0),
        (rows, jnp.where(half == 0, -rows, rows)),
        (mem_rows, rows * half + mem_rows),
    ):
        length = width + rows
        lane = jnp.arange(length, dtype=jnp.int32)
        pieces.append(off + jnp.where(lane < width, -lane, length - lane))
    return bucket_of(jnp.concatenate(pieces))


def mask_lanes(bucket, doc_len, perm_rank, seg_ids, mem_seg):
    slot_rows = perm_rank.shape[0]
    mem_rows = mem_seg.shape[0]
    docs = doc_len.shape[0]
    positions = jnp.arange(slot_rows, dtype=jnp.int32)
    document = positions // bucket
    within = positions - document * bucket
    doc_index = jnp.arange(docs, dtype=jnp.int32)
    doc_length = jnp.sum(
        jnp.where(document[:, None] == doc_index[None, :], doc_len[None, :], 0), axis=1, dtype=jnp.int32
    )
    absent = within >= doc_length
    order = jnp.where(within < 2, 0, jnp.maximum(perm_rank - target_floor, 0))
    lane = jnp.arange(HDIM, dtype=jnp.int32)[None, :]
    slot_order = lane - 6
    slot_doc = lane - 6 - ORDERS
    in_order = (slot_order >= 0) & (slot_order < ORDERS)
    in_doc = (slot_doc >= 0) & (slot_doc < docs)
    is_absent = lane == 6 + ORDERS + docs
    one = (lane == 4) | (lane == 5)
    hide_doc = in_doc & (slot_doc != document[:, None])
    hide_content = in_order & (slot_order > order[:, None])
    hide_query = in_order & (slot_order >= order[:, None]) & (slot_order > 0)

    def query_side(hide):
        return jnp.where(one, 1.0, jnp.where(hide | hide_doc | is_absent, masked_score, 0.0))

    query_lanes = jnp.stack([query_side(hide_content), query_side(hide_query)])
    seg_lane = (lane == 2) | (lane == 3)
    ones_lane = lane < 2

    def key_side(segment, extra):
        return jnp.where(ones_lane, 1.0, jnp.where(seg_lane, segment[:, None].astype(f32), extra))

    token_hot = (
        (in_order & (slot_order == order[:, None]))
        | (in_doc & (slot_doc == document[:, None]))
        | (is_absent & absent[:, None])
    )
    key_lanes = key_side(seg_ids, token_hot.astype(f32))
    mem_lanes = key_side(mem_seg, jnp.zeros((mem_rows, HDIM), f32))

    def both(values_in):
        return jnp.concatenate([values_in, values_in], axis=-1).astype(bf16)

    return both(query_lanes), both(key_lanes), both(mem_lanes)


def split_pair(values_in):
    high = values_in.astype(bf16)
    return high, (values_in - high.astype(f32)).astype(bf16)


def head_tables(content_bias, seg_bias, seg_embed):
    heads = content_bias.shape[0]
    parity = (jnp.arange(heads) % 2)[:, None, None]
    row = jnp.arange(LANES)[None, :, None]
    lane = jnp.arange(LANES)[None, None, :]
    own_row = (row // HDIM) == parity
    spare = (lane // HDIM) != parity
    column = lane % HDIM

    def spread(vectors, lanes):
        tall = jnp.concatenate([vectors, vectors], axis=1)[:, :, None]
        keep = own_row & spare & ((column == lanes[0]) | (column == lanes[1]))
        parts = split_pair(tall)
        return jnp.concatenate([jnp.where(keep, part, jnp.zeros((), bf16)) for part in parts], axis=1)

    first, second = seg_embed[0], seg_embed[1]
    same_seg_one = spread(first, (0, 1)) + spread(second - first, (2, 3))
    same_seg_zero = spread(second, (0, 1)) + spread(first - second, (2, 3))
    seg_table = jnp.concatenate([same_seg_one, same_seg_zero], axis=2)
    key_table = spread(content_bias * SCALE, (4, 5))
    dots = [jnp.sum(seg_bias * part, axis=-1)[:, None] * SCALE for part in (first, second)]
    column = column[:, 0]
    spare = spare[:, 0]

    def const_row(start, slope):
        return jnp.where(spare & (column < 2), start, jnp.where(spare & (column >= 2) & (column < 4), slope, 0.0))

    seg_const = jnp.stack(
        [const_row(dots[0], dots[1] - dots[0]), const_row(dots[1], dots[0] - dots[1])], axis=1
    )
    return seg_table, seg_const, key_table


def nt(left, right):
    return lax.dot_general(left, right, (((1,), (1,)), ((), ())), preferred_element_type=f32)


def nn(left, right):
    return lax.dot_general(left, right, (((1,), (0,)), ((), ())), preferred_element_type=f32)


def tn(left, right):
    return lax.dot_general(left, right, (((0,), (0,)), ((), ())), preferred_element_type=f32)


def lane_of(shape):
    return lax.broadcasted_iota(jnp.int32, shape, len(shape) - 1)


def high_low(values_in, lane):
    high = values_in.astype(bf16).astype(f32)
    return jnp.where(lane % 2 == 0, high, values_in - high)


def attend_kernel(
    full_ref, q_ref, ko_ref, vo_ref, ke_ref, ve_ref, qm_ref, kmo_ref, kme_ref, seg_ref,
    st_ref, sc_ref, kt_ref, diag_ref,
    a_ref, po_ref, pe_ref,
    bo_ref, be_ref,
):
    slot = pl.program_id(1)
    rows = q_ref.shape[2]
    mem_rows = ke_ref.shape[1] - rows

    @pl.when(slot == 0)
    def _():
        for head in range(2):
            start = 0
            for ref, at, width in ((bo_ref, 0, rows), (be_ref, 0, rows), (be_ref, rows, mem_rows)):
                length = width + rows
                line = jnp.broadcast_to(diag_ref[head, :, start : start + length], (rows, length))
                skew = pltpu.roll(line, 0, 1, stride=1, stride_axis=0)
                ref[head, :, at : at + width] = skew[:, :width] * SCALE
                start += length

    lane = lane_of((rows, LANES))
    eye = lax.broadcasted_iota(jnp.int32, (rows, rows), 0) == lax.broadcasted_iota(jnp.int32, (rows, rows), 1)

    def keys_of(k_ref, km_ref, head):
        key_rows = k_ref[0]
        key_lane = lane_of(key_rows.shape)
        shift = nn(jnp.concatenate([key_rows, key_rows], axis=1), kt_ref[head])
        spare = high_low(shift, key_lane) + km_ref[0].astype(f32)
        return jnp.where(key_lane // HDIM == head, key_rows.astype(f32), spare).astype(bf16)

    def run(full):
        keys = [
            (keys_of(ko_ref, kmo_ref, head), keys_of(ke_ref, kme_ref, head) if full else None)
            for head in range(2)
        ]
        for stream in range(2):
            outs = []
            for head in range(2):
                own = lane // HDIM == head
                scaled = q_ref[0, stream] * jnp.asarray(SCALE, bf16)
                table = nn(jnp.concatenate([scaled, scaled], axis=1), st_ref[head])
                seg = jnp.where(
                    seg_ref[0] > 0,
                    table[:, :LANES] + sc_ref[head, 0:1],
                    table[:, LANES:] + sc_ref[head, 1:2],
                )
                spare = high_low(seg, lane) + qm_ref[0, stream].astype(f32)
                queries = jnp.where(own, scaled.astype(f32), spare).astype(bf16)
                key_own, key_ext = keys[head]
                score_own = nt(queries, key_own)
                if stream == 0:
                    plain = own | (lane % HDIM < 6)
                    product = jnp.where(plain, queries.astype(f32) * key_own.astype(f32), 0.0)
                    self_score = jnp.sum(product, axis=1, keepdims=True)
                else:
                    self_score = masked_score
                score_own = jnp.where(eye, self_score, score_own) + bo_ref[head]
                top = jnp.max(score_own, axis=1, keepdims=True)
                if full:
                    score_ext = nt(queries, key_ext) + be_ref[head]
                    top = jnp.maximum(top, jnp.max(score_ext, axis=1, keepdims=True))
                part_own = jnp.exp(score_own - top)
                total = jnp.sum(part_own, axis=1, keepdims=True)
                if full:
                    part_ext = jnp.exp(score_ext - top)
                    total = total + jnp.sum(part_ext, axis=1, keepdims=True)
                inverse = 1.0 / total
                weight_own = (part_own * inverse).astype(bf16)
                po_ref[0, stream, head] = weight_own
                out = nn(weight_own, vo_ref[0])
                if full:
                    weight_ext = (part_ext * inverse).astype(bf16)
                    pe_ref[0, stream, head] = weight_ext
                    out = out + nn(weight_ext, ve_ref[0])
                outs.append(out)
            a_ref[0, stream] = jnp.where(lane < HDIM, outs[0], outs[1]).astype(bf16)

    is_full = full_ref[slot] > 0

    @pl.when(is_full)
    def _():
        run(True)

    @pl.when(jnp.logical_not(is_full))
    def _():
        run(False)


def specs_of(rows, ext):
    by_pair = pl.BlockSpec((1, 2, rows, LANES), lambda p, s, *_: (s, 0, 0, p))
    own = pl.BlockSpec((1, rows, LANES), lambda p, s, *_: (s, 0, p))
    far = pl.BlockSpec((1, ext, LANES), lambda p, s, *_: (s, 0, p))
    own_lanes = pl.BlockSpec((1, rows, LANES), lambda p, s, *_: (s, 0, 0))
    far_lanes = pl.BlockSpec((1, ext, LANES), lambda p, s, *_: (s, 0, 0))
    query_lanes = pl.BlockSpec((1, 2, rows, LANES), lambda p, s, *_: (s, 0, 0, 0))
    weight_own = pl.BlockSpec((1, 2, 2, rows, rows), lambda p, s, *_: (s, 0, p, 0, 0))
    weight_far = pl.BlockSpec((1, 2, 2, rows, ext), lambda p, s, *_: (s, 0, p, 0, 0))
    return by_pair, own, far, own_lanes, far_lanes, query_lanes, weight_own, weight_far


def per_head(*shape):
    return pl.BlockSpec((2,) + shape, lambda p, s, *_: (p,) + (0,) * len(shape))


def attend(full, queries, key_own, value_own, key_ext, value_ext, lanes, tables, diagonals):
    slots, streams, rows, width = queries.shape
    ext = key_ext.shape[1]
    heads = width // HDIM
    query_lanes, own_lanes, ext_lanes, seg_rows = lanes
    seg_table, seg_const, key_table = tables
    pair, own, far, own_l, far_l, query_l, w_own, w_far = specs_of(rows, ext)
    return pl.pallas_call(
        attend_kernel,
        grid_spec=pltpu.PrefetchScalarGridSpec(
            num_scalar_prefetch=1,
            grid=(heads // 2, slots),
            in_specs=[
                pair, own, own, far, far, query_l, own_l, far_l, own_l,
                per_head(2 * LANES, 2 * LANES), per_head(2, LANES), per_head(2 * LANES, LANES),
                per_head(1, diagonals.shape[-1]),
            ],
            out_specs=[pair, w_own, w_far],
            scratch_shapes=[pltpu.VMEM((2, rows, rows), f32), pltpu.VMEM((2, rows, ext), f32)],
        ),
        out_shape=[
            jax.ShapeDtypeStruct(queries.shape, bf16),
            jax.ShapeDtypeStruct((slots, streams, heads, rows, rows), bf16),
            jax.ShapeDtypeStruct((slots, streams, heads, rows, ext), bf16),
        ],
        name="attend",
    )(full, queries, key_own, value_own, key_ext, value_ext, query_lanes, own_lanes, ext_lanes, seg_rows,
      seg_table, seg_const, key_table, diagonals)


def attend_back_kernel(
    full_ref, q_ref, ko_ref, vo_ref, ke_ref, ve_ref, kmo_ref, kme_ref, seg_ref,
    a_ref, da_ref, po_ref, pe_ref, emb_ref, cb_ref,
    dq_ref, dko_ref, dvo_ref, dke_ref, dve_ref, small_ref, diag_ref,
    bo_ref, be_ref,
):
    slot = pl.program_id(1)
    rows = q_ref.shape[2]
    ext = ke_ref.shape[1]
    lane = lane_of((rows, LANES))

    @pl.when(slot == 0)
    def _():
        bo_ref[...] = jnp.zeros_like(bo_ref)
        be_ref[...] = jnp.zeros_like(be_ref)
        small_ref[...] = jnp.zeros_like(small_ref)

    def keys_of(k_ref, km_ref, head):
        key_lane = lane_of(k_ref.shape[1:])
        return jnp.where(key_lane // HDIM == head, k_ref[0], km_ref[0])

    def run(full):
        parts = [(ko_ref, vo_ref, kmo_ref, po_ref, bo_ref, dko_ref, dvo_ref)]
        if full:
            parts.append((ke_ref, ve_ref, kme_ref, pe_ref, be_ref, dke_ref, dve_ref))
        d_queries = [[None, None], [None, None]]
        for head in range(2):
            own = lane // HDIM == head
            base = HDIM * (1 - head)
            key_sets = [keys_of(k_ref, km_ref, head) for k_ref, _, km_ref, *_ in parts]
            d_keys = [0.0] * len(parts)
            d_values = [0.0] * len(parts)
            totals = [jnp.zeros((1, LANES), f32)] * 5
            for stream in range(2):
                queries = q_ref[0, stream]
                flat = jnp.where(
                    own,
                    queries.astype(f32) * SCALE,
                    jnp.where(lane % HDIM == 4, 1.0, 0.0),
                ).astype(bf16)
                cot = jnp.where(own, da_ref[0, stream].astype(f32), 0.0)
                inner = jnp.sum(cot * a_ref[0, stream].astype(f32), axis=1, keepdims=True)
                cot = cot.astype(bf16)
                d_rows = 0.0
                for at, (k_ref, v_ref, km_ref, p_ref, b_ref, dk_ref, dv_ref) in enumerate(parts):
                    weights = p_ref[0, stream, head]
                    d_scores = weights.astype(f32) * (nt(cot, v_ref[0]) - inner)
                    b_ref[head] += d_scores
                    d_scores = d_scores.astype(bf16)
                    d_rows = d_rows + nn(d_scores, key_sets[at])
                    d_keys[at] = d_keys[at] + tn(flat, d_scores)
                    d_values[at] = d_values[at] + tn(cot, weights)
                every = d_rows[:, base : base + 1]
                ones = d_rows[:, base + 2 : base + 3]
                same = jnp.where(seg_ref[0] > 0, ones, every - ones)
                other = every - same
                d_queries[stream][head] = SCALE * (
                    d_rows + other * emb_ref[head, 0:1] + same * emb_ref[head, 1:2]
                )
                wide = queries.astype(f32)
                for row, member in enumerate((other * wide, same * wide, other, same, d_rows)):
                    totals[row] = totals[row] + jnp.sum(member, axis=0, keepdims=True)
            for row in range(5):
                small_ref[head, row : row + 1] += totals[row]
            for at, (k_ref, v_ref, km_ref, p_ref, b_ref, dk_ref, dv_ref) in enumerate(parts):
                column = d_keys[at][base + 4 : base + 5]
                mine = slice(HDIM * head, HDIM * head + HDIM)
                dk_ref[0, mine] = (d_keys[at][mine] + cb_ref[head] * SCALE * column).astype(bf16)
                dv_ref[0, mine] = d_values[at][mine].astype(bf16)
        for stream in range(2):
            dq_ref[0, stream] = jnp.where(lane < HDIM, d_queries[stream][0], d_queries[stream][1]).astype(bf16)

    is_full = full_ref[slot] > 0

    @pl.when(is_full)
    def _():
        run(True)

    @pl.when(jnp.logical_not(is_full))
    def _():
        run(False)
        dke_ref[...] = jnp.zeros_like(dke_ref)
        dve_ref[...] = jnp.zeros_like(dve_ref)

    @pl.when(slot == pl.num_programs(1) - 1)
    def _():
        for head in range(2):
            start = 0
            for ref, at, width in ((bo_ref, 0, rows), (be_ref, 0, rows), (be_ref, rows, ext - rows)):
                length = width + rows
                block = jnp.concatenate([ref[head, :, at : at + width], jnp.zeros((rows, rows), f32)], axis=1)
                step = rows // 2
                while step >= 8:
                    block = block[:step] + pltpu.roll(block[step:], length - step, 1)
                    step //= 2
                diag_ref[head, :, start : start + length] = block
                start += length


def attend_back(
    full, queries, key_own, value_own, key_ext, value_ext, lanes, attended, d_attended, weights,
    seg_rows_embed, bias_columns, diag_length,
):
    slots, streams, rows, width = queries.shape
    ext = key_ext.shape[1]
    heads = width // HDIM
    _, own_lanes, ext_lanes, seg_rows = lanes
    pair, own, far, own_l, far_l, query_l, w_own, w_far = specs_of(rows, ext)
    tall_own = pl.BlockSpec((1, LANES, rows), lambda p, s, *_: (s, p, 0))
    tall_ext = pl.BlockSpec((1, LANES, ext), lambda p, s, *_: (s, p, 0))
    return pl.pallas_call(
        attend_back_kernel,
        grid_spec=pltpu.PrefetchScalarGridSpec(
            num_scalar_prefetch=1,
            grid=(heads // 2, slots),
            in_specs=[
                pair, own, own, far, far, own_l, far_l, own_l, pair, pair, w_own, w_far,
                per_head(2, LANES), per_head(HDIM, 1),
            ],
            out_specs=[pair, tall_own, tall_own, tall_ext, tall_ext, per_head(8, LANES), per_head(8, diag_length)],
            scratch_shapes=[pltpu.VMEM((2, rows, rows), f32), pltpu.VMEM((2, rows, ext), f32)],
        ),
        out_shape=[
            jax.ShapeDtypeStruct(queries.shape, bf16),
            jax.ShapeDtypeStruct((slots, width, rows), bf16),
            jax.ShapeDtypeStruct((slots, width, rows), bf16),
            jax.ShapeDtypeStruct((slots, width, ext), bf16),
            jax.ShapeDtypeStruct((slots, width, ext), bf16),
            jax.ShapeDtypeStruct((heads, 8, LANES), f32),
            jax.ShapeDtypeStruct((heads, 8, diag_length), f32),
        ],
        name="attend_back",
    )(full, queries, key_own, value_own, key_ext, value_ext, own_lanes, ext_lanes, seg_rows,
      attended, d_attended, weights[0], weights[1], seg_rows_embed, bias_columns)


def other_of(values_in):
    size = lax.axis_size("tensor")
    return lax.ppermute(values_in, "tensor", [(i, (i + 1) % size) for i in range(size)])


def in_order(half, mine, other, axis):
    first = jnp.where(half == 0, mine, other)
    second = jnp.where(half == 0, other, mine)
    return jnp.concatenate([first, second], axis=axis)


def gather_rows(values_in):
    parts = lax.axis_size("dp")
    rows = values_in.shape[0] // parts
    piece = lax.dynamic_slice_in_dim(values_in, lax.axis_index("dp") * rows, rows, 0)
    whole = lax.all_gather(piece, ("tensor", "dp"), axis=0, tiled=True)
    return whole.reshape((lax.axis_size("tensor"),) + values_in.shape)


def sum_rows(parts):
    halves, rows, columns = parts.shape
    dp = lax.axis_size("dp")
    pad = -rows % (8 * dp)
    if pad:
        parts = jnp.pad(parts, ((0, 0), (0, pad), (0, 0)))
    flat = parts.astype(bf16).reshape(-1, columns)
    piece = lax.psum_scatter(flat, ("tensor", "dp"), scatter_dimension=0, tiled=True)
    return lax.all_gather(piece, "dp", axis=0, tiled=True)[:rows].astype(f32)


def norm_parts(values_in):
    centred = values_in - jnp.mean(values_in, axis=-1, keepdims=True)
    spread = jnp.mean(centred * centred, axis=-1, keepdims=True)
    return centred, lax.rsqrt(spread + epsilon)


def norm_back(cotangent, gain, centred, inverse):
    unit = centred * inverse
    scaled = cotangent * gain
    first = jnp.mean(scaled, axis=-1, keepdims=True)
    second = jnp.mean(scaled * unit, axis=-1, keepdims=True)
    return inverse * (scaled - first - unit * second), unit


def gelu_pair(values_in):
    rate = 0.7978845608028654
    square = values_in * values_in
    bent = jnp.tanh(rate * values_in * (1.0 + 0.044715 * square))
    half = 0.5 * (1.0 + bent)
    slope = half + 0.5 * values_in * (1.0 - bent * bent) * rate * (1.0 + 3 * 0.044715 * square)
    return values_in * half, slope


def dot_to(equation, left, right):
    return jnp.einsum(equation, left, right, preferred_element_type=f32)


def per_device(
    h_in, g_in, mem_in, d_h_out, d_g_out, w_query, w_key, w_value, w_out, content_bias, seg_bias,
    seg_embed, rel_table, norm1_gain, norm1_bias, w_in, b_in, w_ffo, b_ffo, norm2_gain, norm2_bias,
    bucket_len, doc_len, seg_ids, mem_seg, perm_rank,
):
    half = lax.axis_index("tensor")
    content, stream, memory = h_in[0], g_in[0], mem_in[0]
    slots, rows, width = content.shape
    mem_half = memory.shape[1]
    slot_rows = perm_rank.shape[2]
    mem_rows = mem_seg.shape[2]
    heads_half = w_query.shape[1] // HDIM

    other_rows = other_of(jnp.concatenate([content, memory], axis=1))
    table_half = jnp.concatenate(
        [content_bias, seg_bias, seg_embed[0], seg_embed[1], rel_table], axis=1
    )
    small_half = jnp.concatenate([table_half.reshape(-1), b_in])
    small_other = other_of(small_half)
    cut = table_half.size
    tables = in_order(half, table_half, small_other[:cut].reshape(table_half.shape), 0)
    hidden_bias = in_order(half, b_in, small_other[cut:], 0)
    content_all, seg_all = tables[:, :HDIM], tables[:, HDIM : 2 * HDIM]
    embed_all = jnp.stack([tables[:, 2 * HDIM : 3 * HDIM], tables[:, 3 * HDIM : 4 * HDIM]])
    rel_all = tables[:, 4 * HDIM :]
    heads = rel_all.shape[0]
    wq, wk, wv = gather_rows(w_query), gather_rows(w_key), gather_rows(w_value)
    w_out_all = gather_rows(w_out).reshape(-1, width)
    w_in_all = gather_rows(w_in)
    w_ffo_all = gather_rows(w_ffo).reshape(-1, width)

    full = (bucket_len[0] == slot_rows).astype(jnp.int32)
    query_lanes, key_lanes, mem_lanes = jax.vmap(mask_lanes)(
        bucket_len[0], doc_len[0], perm_rank[0], seg_ids[0], mem_seg[0]
    )
    start = half * rows
    far = slot_rows - rows - start

    def own_of(values_in, axis):
        return lax.dynamic_slice_in_dim(values_in, start, rows, axis)

    seg_rows = jnp.broadcast_to(
        own_of(seg_ids[0], 1).astype(f32)[:, :, None], (slots, rows, LANES)
    )
    lanes = (
        own_of(query_lanes, 2),
        own_of(key_lanes, 1),
        jnp.concatenate([lax.dynamic_slice_in_dim(key_lanes, far, rows, 1), mem_lanes], axis=1),
        seg_rows,
    )
    head_set = head_tables(content_all, seg_all, embed_all)
    buckets = diagonal_buckets(half, rows, mem_rows)
    hot = (buckets[None] == jnp.arange(NREL, dtype=jnp.int32)[:, None]).astype(f32)
    diagonals = jnp.dot(rel_all, hot, precision=highest)[:, None]

    pair = jnp.stack([content, stream], axis=1)

    def project(values_in, weight):
        out = dot_to("sjd,tde->sjte", values_in, weight)
        return out.reshape(values_in.shape[:-1] + (-1,)).astype(bf16)

    flat_pair = pair.reshape(slots, 2 * rows, width)
    queries = project(flat_pair, wq).reshape(slots, 2, rows, -1)
    ext_rows = jnp.concatenate(
        [other_rows[:, :rows], in_order(half, memory, other_rows[:, rows:], 1)], axis=1
    )
    key_own, value_own = project(content, wk), project(content, wv)
    key_ext, value_ext = project(ext_rows, wk), project(ext_rows, wv)

    attended, weight_own, weight_ext = attend(
        full, queries, key_own, value_own, key_ext, value_ext, lanes, head_set, diagonals
    )

    flat_rows = slots * 2 * rows
    attended_flat = attended.reshape(flat_rows, width)
    mid = pair.reshape(flat_rows, width).astype(f32) + dot_to("re,ed->rd", attended_flat, w_out_all)
    centred1, inverse1 = norm_parts(mid)
    normed = centred1 * inverse1 * norm1_gain + norm1_bias
    normed_low = normed.astype(bf16)
    ff_half = w_in.shape[1]
    hidden = dot_to("rd,tdf->rtf", normed_low, w_in_all).reshape(flat_rows, -1) + hidden_bias
    active, slope = gelu_pair(hidden)
    active = active.astype(bf16)
    second = normed + dot_to("rf,fd->rd", active, w_ffo_all) + b_ffo
    centred2, inverse2 = norm_parts(second)
    outputs = (centred2 * inverse2 * norm2_gain + norm2_bias).astype(bf16).reshape(pair.shape)

    cot = jnp.stack([d_h_out[0], d_g_out[0]], axis=1).reshape(flat_rows, width).astype(f32)
    d_second, unit2 = norm_back(cot, norm2_gain, centred2, inverse2)
    d_norm2_gain = jnp.sum(cot * unit2, axis=0)
    d_norm2_bias = jnp.sum(cot, axis=0)
    d_ffn = d_second.astype(bf16)
    d_b_ffo = jnp.sum(d_ffn.astype(f32), axis=0)
    d_w_ffo = dot_to("rf,rd->fd", active, d_ffn)
    d_hidden = (dot_to("rd,fd->rf", d_ffn, w_ffo_all) * slope).astype(bf16)
    d_b_in = jnp.sum(d_hidden.astype(f32), axis=0)
    d_w_in = dot_to("rf,rd->fd", d_hidden, normed_low)
    ffn_sums = sum_rows(
        jnp.concatenate(
            [member.astype(bf16).reshape(2, ff_half, width) for member in (d_w_ffo, d_w_in)], axis=1
        )
    )
    d_normed = d_second + dot_to("rtf,tdf->rd", d_hidden.reshape(flat_rows, 2, ff_half), w_in_all)
    d_mid, unit1 = norm_back(d_normed, norm1_gain, centred1, inverse1)
    d_norm1_gain = jnp.sum(d_normed * unit1, axis=0)
    d_norm1_bias = jnp.sum(d_normed, axis=0)
    d_attn = d_mid.astype(bf16)
    d_w_out = dot_to("re,rd->ed", attended_flat, d_attn)
    d_attended = dot_to("rd,ed->re", d_attn, w_out_all).astype(bf16).reshape(attended.shape)

    embed_rows = jnp.transpose(embed_all, (1, 0, 2))
    embed_rows = jnp.concatenate([embed_rows, embed_rows], axis=-1)
    d_query, dk_own, dv_own, dk_ext, dv_ext, small, diag = attend_back(
        full, queries, key_own, value_own, key_ext, value_ext, lanes, attended, d_attended,
        (weight_own, weight_ext), embed_rows, content_all[:, :, None], diagonals.shape[-1],
    )
    aligned = []
    begin = 0
    for block in (rows, rows, mem_rows):
        piece = diag[:, :, begin : begin + block + rows]
        begin += block + rows
        aligned.append(sum(jnp.roll(piece[:, step], -step, axis=-1) for step in range(piece.shape[1])))
    d_rel = jnp.einsum("hl,rl->hr", jnp.concatenate(aligned, -1), hot, precision=highest) * SCALE
    odd = (jnp.arange(heads) % 2)[:, None, None]
    small = jnp.where(odd == 0, small[:, :, :HDIM], small[:, :, HDIM:]) * SCALE
    d_content_bias = small[:, 4]
    d_embed = [small[:, c] + small[:, 2 + c] * seg_all for c in range(2)]
    d_seg_bias = small[:, 2] * embed_all[0] + small[:, 3] * embed_all[1]

    pair_flat = pair.reshape(flat_rows, width)
    d_query_flat = d_query.reshape(flat_rows, width)
    d_wq = dot_to("re,rd->ed", d_query_flat, pair_flat)
    d_wk = dot_to("sej,sjd->ed", dk_own, content) + dot_to("sej,sjd->ed", dk_ext, ext_rows)
    d_wv = dot_to("sej,sjd->ed", dv_own, content) + dot_to("sej,sjd->ed", dv_ext, ext_rows)
    head_small = jnp.concatenate(
        [d_content_bias, d_seg_bias, d_embed[0], d_embed[1], d_rel], axis=1
    ).reshape(2, -1)
    shared = jnp.concatenate([d_norm1_gain, d_norm1_bias, d_norm2_gain, d_norm2_bias, d_b_ffo])
    smalls = jnp.concatenate(
        [jnp.broadcast_to(shared, (2,) + shared.shape), d_b_in.reshape(2, -1), head_small], axis=1
    )
    small_size = smalls.shape[1]
    smalls = jnp.pad(smalls, ((0, 0), (0, -small_size % width)))
    heads_width = width // 2
    proj_sums = sum_rows(
        jnp.concatenate(
            [member.astype(bf16).reshape(2, heads_width, width) for member in (d_wq, d_wk, d_wv, d_w_out)]
            + [smalls.astype(bf16).reshape(2, -1, width)],
            axis=1,
        )
    )

    def back_keys(dk, dv):
        def part(d_rows, weight):
            split = d_rows.reshape(slots, 2, -1, d_rows.shape[-1])
            return dot_to("stej,tde->sjd", split, weight)

        return part(dk, wk) + part(dv, wv)

    d_ext = back_keys(dk_ext, dv_ext).astype(bf16)
    mem_mine = jnp.where(half == 0, d_ext[:, rows : rows + mem_half], d_ext[:, rows + mem_half :])
    mem_away = jnp.where(half == 0, d_ext[:, rows + mem_half :], d_ext[:, rows : rows + mem_half])
    arrived = other_of(jnp.concatenate([d_ext[:, :rows], mem_away], axis=1)).astype(f32)
    d_pair = (
        d_mid + dot_to("rte,tde->rd", d_query_flat.reshape(flat_rows, 2, heads_width), wq)
    ).reshape(slots, 2, rows, width)
    d_content = d_pair[:, 0] + back_keys(dk_own, dv_own) + arrived[:, :rows]
    d_memory = mem_mine.astype(f32) + arrived[:, rows:]

    def take(values_in, at, shape):
        size = 1
        for extent in shape:
            size *= extent
        return values_in[at : at + size].reshape(shape), at + size

    small_sum = proj_sums[4 * heads_width :].reshape(-1)[:small_size]
    at = 0
    vectors = []
    for _ in range(5):
        vector, at = take(small_sum, at, (width,))
        vectors.append(vector)
    sum_b_in, at = take(small_sum, at, (ff_half,))
    per_head_sums, at = take(small_sum, at, (heads_half, 4 * HDIM + NREL))
    d_small = [per_head_sums[:, HDIM * c : HDIM * (c + 1)] for c in range(4)]
    blocks = [proj_sums[heads_width * c : heads_width * (c + 1)] for c in range(4)]
    return (
        outputs[:, 0][None],
        outputs[:, 1][None],
        d_content.astype(bf16)[None],
        d_pair[:, 1].astype(bf16)[None],
        d_memory.astype(bf16)[None],
        blocks[0].T,
        blocks[1].T,
        blocks[2].T,
        blocks[3],
        d_small[0],
        d_small[1],
        jnp.stack([d_small[2], d_small[3]]),
        per_head_sums[:, 4 * HDIM :],
        vectors[0],
        vectors[1],
        ffn_sums[ff_half:].T,
        sum_b_in,
        ffn_sums[:ff_half],
        vectors[4],
        vectors[2],
        vectors[3],
    )


def solution(mesh):
    rows = P("dp", None, "tensor", None)
    columns = P(None, "tensor")
    lead = P("tensor", None)
    group = P("dp", None, None)
    return jax.shard_map(
        per_device,
        mesh=mesh,
        in_specs=(
            rows, rows, rows, rows, rows, columns, columns, columns, lead, lead, lead,
            P(None, "tensor", None), lead, P(), P(), columns, P("tensor"), lead, P(), P(), P(),
            P("dp", None), group, group, group, group,
        ),
        out_specs=(
            rows, rows, rows, rows, rows, columns, columns, columns, lead, lead, lead,
            P(None, "tensor", None), lead, P(), P(), columns, P("tensor"), lead, P(), P(), P(),
        ),
        check_vma=False,
    )
```

```python
import jax
import jax.numpy as jnp
from jax import lax
from jax.experimental import pallas as pl
from jax.experimental.pallas import tpu as pltpu
from jax.sharding import PartitionSpec as P

HDIM = 64
NREL = 32
epsilon = 1e-05
masked_score = -1e30
target_floor = 48
distance_steps = (1, 2, 3, 4, 5, 6, 7, 8, 12, 16, 24, 32, 64, 128, 256)
highest = lax.Precision.HIGHEST
f32 = jnp.float32
bf16 = jnp.bfloat16
LANES = 128
ORDERS = 16
SCALE = HDIM ** (-0.5)


def bucket_of(distance):
    magnitude = jnp.abs(distance)
    counted = jnp.zeros(distance.shape, jnp.int32)
    for threshold in distance_steps:
        counted = counted + (magnitude >= threshold).astype(jnp.int32)
    return counted + NREL // 2 * (distance > 0).astype(jnp.int32)


def diagonal_buckets(half, rows, mem_rows):
    pieces = []
    for width, off in (
        (rows, 0),
        (rows, jnp.where(half == 0, -rows, rows)),
        (mem_rows, rows * half + mem_rows),
    ):
        length = width + rows
        lane = jnp.arange(length, dtype=jnp.int32)
        pieces.append(off + jnp.where(lane < width, -lane, length - lane))
    return bucket_of(jnp.concatenate(pieces))


def mask_lanes(bucket, doc_len, perm_rank, seg_ids, mem_seg):
    slot_rows = perm_rank.shape[0]
    mem_rows = mem_seg.shape[0]
    docs = doc_len.shape[0]
    positions = jnp.arange(slot_rows, dtype=jnp.int32)
    document = positions // bucket
    within = positions - document * bucket
    doc_index = jnp.arange(docs, dtype=jnp.int32)
    doc_length = jnp.sum(
        jnp.where(document[:, None] == doc_index[None, :], doc_len[None, :], 0), axis=1, dtype=jnp.int32
    )
    absent = within >= doc_length
    order = jnp.where(within < 2, 0, jnp.maximum(perm_rank - target_floor, 0))
    lane = jnp.arange(HDIM, dtype=jnp.int32)[None, :]
    slot_order = lane - 6
    slot_doc = lane - 6 - ORDERS
    in_order = (slot_order >= 0) & (slot_order < ORDERS)
    in_doc = (slot_doc >= 0) & (slot_doc < docs)
    is_absent = lane == 6 + ORDERS + docs
    one = (lane == 4) | (lane == 5)
    hide_doc = in_doc & (slot_doc != document[:, None])
    hide_content = in_order & (slot_order > order[:, None])
    hide_query = in_order & (slot_order >= order[:, None]) & (slot_order > 0)

    def query_side(hide):
        return jnp.where(one, 1.0, jnp.where(hide | hide_doc | is_absent, masked_score, 0.0))

    query_lanes = jnp.stack([query_side(hide_content), query_side(hide_query)])
    seg_lane = (lane == 2) | (lane == 3)
    ones_lane = lane < 2

    def key_side(segment, extra):
        return jnp.where(ones_lane, 1.0, jnp.where(seg_lane, segment[:, None].astype(f32), extra))

    token_hot = (
        (in_order & (slot_order == order[:, None]))
        | (in_doc & (slot_doc == document[:, None]))
        | (is_absent & absent[:, None])
    )
    key_lanes = key_side(seg_ids, token_hot.astype(f32))
    mem_lanes = key_side(mem_seg, jnp.zeros((mem_rows, HDIM), f32))

    def both(values_in):
        return jnp.concatenate([values_in, values_in], axis=-1).astype(bf16)

    return both(query_lanes), both(key_lanes), both(mem_lanes)


def split_pair(values_in):
    high = values_in.astype(bf16)
    return high, (values_in - high.astype(f32)).astype(bf16)


def head_tables(content_bias, seg_bias, seg_embed):
    heads = content_bias.shape[0]
    parity = (jnp.arange(heads) % 2)[:, None, None]
    row = jnp.arange(LANES)[None, :, None]
    lane = jnp.arange(LANES)[None, None, :]
    own_row = (row // HDIM) == parity
    spare = (lane // HDIM) != parity
    column = lane % HDIM

    def spread(vectors, lanes):
        tall = jnp.concatenate([vectors, vectors], axis=1)[:, :, None]
        keep = own_row & spare & ((column == lanes[0]) | (column == lanes[1]))
        parts = split_pair(tall)
        return jnp.concatenate([jnp.where(keep, part, jnp.zeros((), bf16)) for part in parts], axis=1)

    first, second = seg_embed[0], seg_embed[1]
    same_seg_one = spread(first, (0, 1)) + spread(second - first, (2, 3))
    same_seg_zero = spread(second, (0, 1)) + spread(first - second, (2, 3))
    seg_table = jnp.concatenate([same_seg_one, same_seg_zero], axis=2)
    key_table = spread(content_bias * SCALE, (4, 5))
    dots = [jnp.sum(seg_bias * part, axis=-1)[:, None] * SCALE for part in (first, second)]
    column = column[:, 0]
    spare = spare[:, 0]

    def const_row(start, slope):
        return jnp.where(spare & (column < 2), start, jnp.where(spare & (column >= 2) & (column < 4), slope, 0.0))

    seg_const = jnp.stack(
        [const_row(dots[0], dots[1] - dots[0]), const_row(dots[1], dots[0] - dots[1])], axis=1
    )
    return seg_table, seg_const, key_table


def nt(left, right):
    return lax.dot_general(left, right, (((1,), (1,)), ((), ())), preferred_element_type=f32)


def nn(left, right):
    return lax.dot_general(left, right, (((1,), (0,)), ((), ())), preferred_element_type=f32)


def tn(left, right):
    return lax.dot_general(left, right, (((0,), (0,)), ((), ())), preferred_element_type=f32)


def lane_of(shape):
    return lax.broadcasted_iota(jnp.int32, shape, len(shape) - 1)


def high_low(values_in, lane):
    high = values_in.astype(bf16).astype(f32)
    return jnp.where(lane % 2 == 0, high, values_in - high)


def attend_kernel(
    full_ref, q_ref, ko_ref, vo_ref, ke_ref, ve_ref, qm_ref, kmo_ref, kme_ref, seg_ref,
    st_ref, sc_ref, kt_ref, diag_ref,
    a_ref, po_ref, pe_ref,
    bo_ref, be_ref,
):
    slot = pl.program_id(1)
    rows = q_ref.shape[2]
    mem_rows = ke_ref.shape[1] - rows

    @pl.when(slot == 0)
    def _():
        for head in range(2):
            start = 0
            for ref, at, width in ((bo_ref, 0, rows), (be_ref, 0, rows), (be_ref, rows, mem_rows)):
                length = width + rows
                line = jnp.broadcast_to(diag_ref[head, :, start : start + length], (rows, length))
                skew = pltpu.roll(line, 0, 1, stride=1, stride_axis=0)
                ref[head, :, at : at + width] = skew[:, :width] * SCALE
                start += length

    lane = lane_of((rows, LANES))
    eye = lax.broadcasted_iota(jnp.int32, (rows, rows), 0) == lax.broadcasted_iota(jnp.int32, (rows, rows), 1)

    def keys_of(k_ref, km_ref, head):
        key_rows = k_ref[0]
        key_lane = lane_of(key_rows.shape)
        shift = nn(jnp.concatenate([key_rows, key_rows], axis=1), kt_ref[head])
        spare = high_low(shift, key_lane) + km_ref[0].astype(f32)
        return jnp.where(key_lane // HDIM == head, key_rows.astype(f32), spare).astype(bf16)

    def run(full):
        keys = [
            (keys_of(ko_ref, kmo_ref, head), keys_of(ke_ref, kme_ref, head) if full else None)
            for head in range(2)
        ]
        for stream in range(2):
            outs = []
            for head in range(2):
                own = lane // HDIM == head
                scaled = q_ref[0, stream] * jnp.asarray(SCALE, bf16)
                table = nn(jnp.concatenate([scaled, scaled], axis=1), st_ref[head])
                seg = jnp.where(
                    seg_ref[0] > 0,
                    table[:, :LANES] + sc_ref[head, 0:1],
                    table[:, LANES:] + sc_ref[head, 1:2],
                )
                spare = high_low(seg, lane) + qm_ref[0, stream].astype(f32)
                queries = jnp.where(own, scaled.astype(f32), spare).astype(bf16)
                key_own, key_ext = keys[head]
                score_own = nt(queries, key_own)
                if stream == 0:
                    plain = own | (lane % HDIM < 6)
                    product = jnp.where(plain, queries.astype(f32) * key_own.astype(f32), 0.0)
                    self_score = jnp.sum(product, axis=1, keepdims=True)
                else:
                    self_score = masked_score
                score_own = jnp.where(eye, self_score, score_own) + bo_ref[head]
                top = jnp.max(score_own, axis=1, keepdims=True)
                if full:
                    score_ext = nt(queries, key_ext) + be_ref[head]
                    top = jnp.maximum(top, jnp.max(score_ext, axis=1, keepdims=True))
                part_own = jnp.exp(score_own - top)
                total = jnp.sum(part_own, axis=1, keepdims=True)
                if full:
                    part_ext = jnp.exp(score_ext - top)
                    total = total + jnp.sum(part_ext, axis=1, keepdims=True)
                inverse = 1.0 / total
                weight_own = (part_own * inverse).astype(bf16)
                po_ref[0, stream, head] = weight_own
                out = nn(weight_own, vo_ref[0])
                if full:
                    weight_ext = (part_ext * inverse).astype(bf16)
                    pe_ref[0, stream, head] = weight_ext
                    out = out + nn(weight_ext, ve_ref[0])
                outs.append(out)
            a_ref[0, stream] = jnp.where(lane < HDIM, outs[0], outs[1]).astype(bf16)

    is_full = full_ref[slot] > 0

    @pl.when(is_full)
    def _():
        run(True)

    @pl.when(jnp.logical_not(is_full))
    def _():
        run(False)


def specs_of(rows, ext):
    by_pair = pl.BlockSpec((1, 2, rows, LANES), lambda p, s, *_: (s, 0, 0, p))
    own = pl.BlockSpec((1, rows, LANES), lambda p, s, *_: (s, 0, p))
    far = pl.BlockSpec((1, ext, LANES), lambda p, s, *_: (s, 0, p))
    own_lanes = pl.BlockSpec((1, rows, LANES), lambda p, s, *_: (s, 0, 0))
    far_lanes = pl.BlockSpec((1, ext, LANES), lambda p, s, *_: (s, 0, 0))
    query_lanes = pl.BlockSpec((1, 2, rows, LANES), lambda p, s, *_: (s, 0, 0, 0))
    weight_own = pl.BlockSpec((1, 2, 2, rows, rows), lambda p, s, *_: (s, 0, p, 0, 0))
    weight_far = pl.BlockSpec((1, 2, 2, rows, ext), lambda p, s, *_: (s, 0, p, 0, 0))
    return by_pair, own, far, own_lanes, far_lanes, query_lanes, weight_own, weight_far


def per_head(*shape):
    return pl.BlockSpec((2,) + shape, lambda p, s, *_: (p,) + (0,) * len(shape))


def attend(full, queries, key_own, value_own, key_ext, value_ext, lanes, tables, diagonals):
    slots, streams, rows, width = queries.shape
    ext = key_ext.shape[1]
    heads = width // HDIM
    query_lanes, own_lanes, ext_lanes, seg_rows = lanes
    seg_table, seg_const, key_table = tables
    pair, own, far, own_l, far_l, query_l, w_own, w_far = specs_of(rows, ext)
    return pl.pallas_call(
        attend_kernel,
        grid_spec=pltpu.PrefetchScalarGridSpec(
            num_scalar_prefetch=1,
            grid=(heads // 2, slots),
            in_specs=[
                pair, own, own, far, far, query_l, own_l, far_l, own_l,
                per_head(2 * LANES, 2 * LANES), per_head(2, LANES), per_head(2 * LANES, LANES),
                per_head(1, diagonals.shape[-1]),
            ],
            out_specs=[pair, w_own, w_far],
            scratch_shapes=[pltpu.VMEM((2, rows, rows), f32), pltpu.VMEM((2, rows, ext), f32)],
        ),
        out_shape=[
            jax.ShapeDtypeStruct(queries.shape, bf16),
            jax.ShapeDtypeStruct((slots, streams, heads, rows, rows), bf16),
            jax.ShapeDtypeStruct((slots, streams, heads, rows, ext), bf16),
        ],
        name="attend",
    )(full, queries, key_own, value_own, key_ext, value_ext, query_lanes, own_lanes, ext_lanes, seg_rows,
      seg_table, seg_const, key_table, diagonals)


def attend_back_kernel(
    full_ref, q_ref, ko_ref, vo_ref, ke_ref, ve_ref, kmo_ref, kme_ref, seg_ref,
    a_ref, da_ref, po_ref, pe_ref, emb_ref, cb_ref,
    dq_ref, dko_ref, dvo_ref, dke_ref, dve_ref, small_ref, diag_ref,
    bo_ref, be_ref,
):
    slot = pl.program_id(1)
    rows = q_ref.shape[2]
    ext = ke_ref.shape[1]
    lane = lane_of((rows, LANES))

    @pl.when(slot == 0)
    def _():
        bo_ref[...] = jnp.zeros_like(bo_ref)
        be_ref[...] = jnp.zeros_like(be_ref)
        small_ref[...] = jnp.zeros_like(small_ref)

    def keys_of(k_ref, km_ref, head):
        key_lane = lane_of(k_ref.shape[1:])
        return jnp.where(key_lane // HDIM == head, k_ref[0], km_ref[0])

    def run(full):
        parts = [(ko_ref, vo_ref, kmo_ref, po_ref, bo_ref, dko_ref, dvo_ref)]
        if full:
            parts.append((ke_ref, ve_ref, kme_ref, pe_ref, be_ref, dke_ref, dve_ref))
        d_queries = [[None, None], [None, None]]
        for head in range(2):
            own = lane // HDIM == head
            base = HDIM * (1 - head)
            key_sets = [keys_of(k_ref, km_ref, head) for k_ref, _, km_ref, *_ in parts]
            d_keys = [0.0] * len(parts)
            d_values = [0.0] * len(parts)
            totals = [jnp.zeros((1, LANES), f32)] * 5
            for stream in range(2):
                queries = q_ref[0, stream]
                flat = jnp.where(
                    own,
                    queries.astype(f32) * SCALE,
                    jnp.where(lane % HDIM == 4, 1.0, 0.0),
                ).astype(bf16)
                cot = jnp.where(own, da_ref[0, stream].astype(f32), 0.0)
                inner = jnp.sum(cot * a_ref[0, stream].astype(f32), axis=1, keepdims=True)
                cot = cot.astype(bf16)
                d_rows = 0.0
                for at, (k_ref, v_ref, km_ref, p_ref, b_ref, dk_ref, dv_ref) in enumerate(parts):
                    weights = p_ref[0, stream, head]
                    d_scores = weights.astype(f32) * (nt(cot, v_ref[0]) - inner)
                    b_ref[head] += d_scores
                    d_scores = d_scores.astype(bf16)
                    d_rows = d_rows + nn(d_scores, key_sets[at])
                    d_keys[at] = d_keys[at] + tn(flat, d_scores)
                    d_values[at] = d_values[at] + tn(cot, weights)
                every = d_rows[:, base : base + 1]
                ones = d_rows[:, base + 2 : base + 3]
                same = jnp.where(seg_ref[0] > 0, ones, every - ones)
                other = every - same
                d_queries[stream][head] = SCALE * (
                    d_rows + other * emb_ref[head, 0:1] + same * emb_ref[head, 1:2]
                )
                wide = queries.astype(f32)
                for row, member in enumerate((other * wide, same * wide, other, same, d_rows)):
                    totals[row] = totals[row] + jnp.sum(member, axis=0, keepdims=True)
            for row in range(5):
                small_ref[head, row : row + 1] += totals[row]
            for at, (k_ref, v_ref, km_ref, p_ref, b_ref, dk_ref, dv_ref) in enumerate(parts):
                column = d_keys[at][base + 4 : base + 5]
                mine = slice(HDIM * head, HDIM * head + HDIM)
                dk_ref[0, mine] = (d_keys[at][mine] + cb_ref[head] * SCALE * column).astype(bf16)
                dv_ref[0, mine] = d_values[at][mine].astype(bf16)
        for stream in range(2):
            dq_ref[0, stream] = jnp.where(lane < HDIM, d_queries[stream][0], d_queries[stream][1]).astype(bf16)

    is_full = full_ref[slot] > 0

    @pl.when(is_full)
    def _():
        run(True)

    @pl.when(jnp.logical_not(is_full))
    def _():
        run(False)
        dke_ref[...] = jnp.zeros_like(dke_ref)
        dve_ref[...] = jnp.zeros_like(dve_ref)

    @pl.when(slot == pl.num_programs(1) - 1)
    def _():
        for head in range(2):
            start = 0
            for ref, at, width in ((bo_ref, 0, rows), (be_ref, 0, rows), (be_ref, rows, ext - rows)):
                length = width + rows
                block = jnp.concatenate([ref[head, :, at : at + width], jnp.zeros((rows, rows), f32)], axis=1)
                step = rows // 2
                while step >= 8:
                    block = block[:step] + pltpu.roll(block[step:], length - step, 1)
                    step //= 2
                diag_ref[head, :, start : start + length] = block
                start += length


def attend_back(
    full, queries, key_own, value_own, key_ext, value_ext, lanes, attended, d_attended, weights,
    seg_rows_embed, bias_columns, diag_length,
):
    slots, streams, rows, width = queries.shape
    ext = key_ext.shape[1]
    heads = width // HDIM
    _, own_lanes, ext_lanes, seg_rows = lanes
    pair, own, far, own_l, far_l, query_l, w_own, w_far = specs_of(rows, ext)
    tall_own = pl.BlockSpec((1, LANES, rows), lambda p, s, *_: (s, p, 0))
    tall_ext = pl.BlockSpec((1, LANES, ext), lambda p, s, *_: (s, p, 0))
    return pl.pallas_call(
        attend_back_kernel,
        grid_spec=pltpu.PrefetchScalarGridSpec(
            num_scalar_prefetch=1,
            grid=(heads // 2, slots),
            in_specs=[
                pair, own, own, far, far, own_l, far_l, own_l, pair, pair, w_own, w_far,
                per_head(2, LANES), per_head(HDIM, 1),
            ],
            out_specs=[pair, tall_own, tall_own, tall_ext, tall_ext, per_head(8, LANES), per_head(8, diag_length)],
            scratch_shapes=[pltpu.VMEM((2, rows, rows), f32), pltpu.VMEM((2, rows, ext), f32)],
        ),
        out_shape=[
            jax.ShapeDtypeStruct(queries.shape, bf16),
            jax.ShapeDtypeStruct((slots, width, rows), bf16),
            jax.ShapeDtypeStruct((slots, width, rows), bf16),
            jax.ShapeDtypeStruct((slots, width, ext), bf16),
            jax.ShapeDtypeStruct((slots, width, ext), bf16),
            jax.ShapeDtypeStruct((heads, 8, LANES), f32),
            jax.ShapeDtypeStruct((heads, 8, diag_length), f32),
        ],
        name="attend_back",
    )(full, queries, key_own, value_own, key_ext, value_ext, own_lanes, ext_lanes, seg_rows,
      attended, d_attended, weights[0], weights[1], seg_rows_embed, bias_columns)


def other_of(values_in):
    size = lax.axis_size("tensor")
    return lax.ppermute(values_in, "tensor", [(i, (i + 1) % size) for i in range(size)])


def across(values_in, step):
    return lax.ppermute(values_in, "dp", [(i, i ^ step) for i in range(lax.axis_size("dp"))])


def ordered(bit, mine, other, axis):
    first = jnp.where(bit == 0, mine, other)
    second = jnp.where(bit == 0, other, mine)
    return jnp.concatenate([first, second], axis=axis)


def piece_of(values_in, at, count, axis=0):
    size = values_in.shape[axis] // count
    return lax.dynamic_slice_in_dim(values_in, at * size, size, axis)


def fetch_half(values_in, core, axis):
    near = other_of(piece_of(values_in, core, 2, axis))
    return near, across(near, 1)


def exchange_levels():
    left = lax.axis_size("dp") // 2
    step = 2
    levels = []
    while left > 1:
        count = min(left, 8)
        levels.append((step, count))
        step *= count
        left //= count
    return levels


def sum_rows(mine, away):
    dp = lax.axis_index("dp")
    total = mine.astype(f32) + other_of(away).astype(f32)
    levels = exchange_levels()
    for step, count in levels:
        low = total.astype(bf16)
        digit = (dp // step) % count
        total = piece_of(total, digit, count)
        for offset in range(1, count):
            arrived = across(piece_of(low, digit ^ offset, count), step * offset)
            total = total + arrived.astype(f32)
    low = total.astype(bf16)
    for step, count in reversed(levels):
        digit = (dp // step) % count
        stack = jnp.stack([low] + [across(low, step * offset) for offset in range(1, count)])
        low = jnp.concatenate(
            [lax.dynamic_index_in_dim(stack, digit ^ place, 0, keepdims=False) for place in range(count)]
        )
    return ordered(dp % 2, low, across(low, 1), 0)


def core_sum(own_half, near, far, core):
    sent = jnp.concatenate([piece_of(own_half, 1 - core, 2), far])
    kept = jnp.concatenate([piece_of(own_half, core, 2), near])
    total = (kept.astype(f32) + across(sent, 1).astype(f32)).astype(bf16)
    size = near.shape[0]
    return total[:size], total[size:]


def padded(values_in):
    rows = values_in.shape[-2]
    block = 16 * lax.axis_size("dp")
    return jnp.pad(values_in, [(0, 0)] * (values_in.ndim - 2) + [(0, -rows % block), (0, 0)])


def norm_parts(values_in):
    centred = values_in - jnp.mean(values_in, axis=-1, keepdims=True)
    spread = jnp.mean(centred * centred, axis=-1, keepdims=True)
    return centred, lax.rsqrt(spread + epsilon)


def norm_back(cotangent, gain, centred, inverse):
    unit = centred * inverse
    scaled = cotangent * gain
    first = jnp.mean(scaled, axis=-1, keepdims=True)
    second = jnp.mean(scaled * unit, axis=-1, keepdims=True)
    return inverse * (scaled - first - unit * second), unit


def gelu_pair(values_in):
    rate = 0.7978845608028654
    square = values_in * values_in
    bent = jnp.tanh(rate * values_in * (1.0 + 0.044715 * square))
    half = 0.5 * (1.0 + bent)
    slope = half + 0.5 * values_in * (1.0 - bent * bent) * rate * (1.0 + 3 * 0.044715 * square)
    return values_in * half, slope


def dot_to(equation, left, right):
    return jnp.einsum(equation, left, right, preferred_element_type=f32)


def per_device(
    h_in, g_in, mem_in, d_h_out, d_g_out, w_query, w_key, w_value, w_out, content_bias, seg_bias,
    seg_embed, rel_table, norm1_gain, norm1_bias, w_in, b_in, w_ffo, b_ffo, norm2_gain, norm2_bias,
    bucket_len, doc_len, seg_ids, mem_seg, perm_rank,
):
    half = lax.axis_index("tensor")
    content, stream, memory = h_in[0], g_in[0], mem_in[0]
    slots, rows, width = content.shape
    mem_half = memory.shape[1]
    slot_rows = perm_rank.shape[2]
    mem_rows = mem_seg.shape[2]
    heads_half = w_query.shape[1] // HDIM

    core = lax.axis_index("dp") % 2

    proj_own = jnp.stack([w_query, w_key, w_value])
    proj_far = ordered(core, *fetch_half(proj_own, core, 1), 1)
    wq, wk, wv = [jnp.concatenate([proj_own[c], proj_far[c]], axis=1) for c in range(3)]
    other_rows = other_of(jnp.concatenate([content, memory], axis=1))
    w_out_all = jnp.concatenate([w_out, ordered(core, *fetch_half(w_out, core, 0), 0)], axis=0)
    table_half = jnp.concatenate(
        [content_bias, seg_bias, seg_embed[0], seg_embed[1], rel_table], axis=1
    )
    small_half = jnp.concatenate([table_half.reshape(-1), b_in])
    small_other = other_of(small_half)
    cut = table_half.size
    tables = jnp.concatenate([table_half, small_other[:cut].reshape(table_half.shape)], axis=0)
    content_all, seg_all = tables[:, :HDIM], tables[:, HDIM : 2 * HDIM]
    embed_all = jnp.stack([tables[:, 2 * HDIM : 3 * HDIM], tables[:, 3 * HDIM : 4 * HDIM]])
    rel_all = tables[:, 4 * HDIM :]
    heads = rel_all.shape[0]
    ff_half = w_in.shape[1]
    w_in_near, w_in_far = fetch_half(w_in, core, 1)
    w_in_all = jnp.concatenate([w_in, w_in_near, w_in_far], axis=1)
    w_ffo_near, w_ffo_far = fetch_half(w_ffo, core, 0)
    w_ffo_all = jnp.concatenate([w_ffo, w_ffo_near, w_ffo_far], axis=0)
    bias_other = small_other[cut:]
    hidden_bias = jnp.concatenate(
        [b_in, piece_of(bias_other, core, 2), piece_of(bias_other, 1 - core, 2)]
    )

    full = (bucket_len[0] == slot_rows).astype(jnp.int32)
    query_lanes, key_lanes, mem_lanes = jax.vmap(mask_lanes)(
        bucket_len[0], doc_len[0], perm_rank[0], seg_ids[0], mem_seg[0]
    )
    start = half * rows
    far = slot_rows - rows - start

    def own_of(values_in, axis):
        return lax.dynamic_slice_in_dim(values_in, start, rows, axis)

    seg_rows = jnp.broadcast_to(
        own_of(seg_ids[0], 1).astype(f32)[:, :, None], (slots, rows, LANES)
    )
    lanes = (
        own_of(query_lanes, 2),
        own_of(key_lanes, 1),
        jnp.concatenate([lax.dynamic_slice_in_dim(key_lanes, far, rows, 1), mem_lanes], axis=1),
        seg_rows,
    )
    head_set = head_tables(content_all, seg_all, embed_all)
    buckets = diagonal_buckets(half, rows, mem_rows)
    hot = (buckets[None] == jnp.arange(NREL, dtype=jnp.int32)[:, None]).astype(f32)
    diagonals = jnp.dot(rel_all, hot, precision=highest)[:, None]

    pair = jnp.stack([content, stream], axis=1)

    def project(values_in, weight):
        return dot_to("sjd,de->sje", values_in, weight).astype(bf16)

    flat_pair = pair.reshape(slots, 2 * rows, width)
    queries = project(flat_pair, wq).reshape(slots, 2, rows, -1)
    ext_rows = jnp.concatenate(
        [other_rows[:, :rows], ordered(half, memory, other_rows[:, rows:], 1)], axis=1
    )
    key_own, value_own = project(content, wk), project(content, wv)
    key_ext, value_ext = project(ext_rows, wk), project(ext_rows, wv)

    attended, weight_own, weight_ext = attend(
        full, queries, key_own, value_own, key_ext, value_ext, lanes, head_set, diagonals
    )

    flat_rows = slots * 2 * rows
    attended_flat = attended.reshape(flat_rows, width)
    mid = pair.reshape(flat_rows, width).astype(f32) + dot_to("re,ed->rd", attended_flat, w_out_all)
    centred1, inverse1 = norm_parts(mid)
    normed = centred1 * inverse1 * norm1_gain + norm1_bias
    normed_low = normed.astype(bf16)
    hidden = dot_to("rd,df->rf", normed_low, w_in_all) + hidden_bias
    active, slope = gelu_pair(hidden)
    active = active.astype(bf16)
    second = normed + dot_to("rf,fd->rd", active, w_ffo_all) + b_ffo
    centred2, inverse2 = norm_parts(second)
    outputs = (centred2 * inverse2 * norm2_gain + norm2_bias).astype(bf16).reshape(pair.shape)

    cot = jnp.stack([d_h_out[0], d_g_out[0]], axis=1).reshape(flat_rows, width).astype(f32)
    d_second, unit2 = norm_back(cot, norm2_gain, centred2, inverse2)
    d_norm2_gain = jnp.sum(cot * unit2, axis=0)
    d_norm2_bias = jnp.sum(cot, axis=0)
    d_ffn = d_second.astype(bf16)
    d_b_ffo = jnp.sum(d_ffn.astype(f32), axis=0)
    d_w_ffo = dot_to("rf,rd->fd", active, d_ffn)
    d_hidden = (dot_to("rd,fd->rf", d_ffn, w_ffo_all) * slope).astype(bf16)
    d_b_in = jnp.sum(d_hidden.astype(f32), axis=0)
    d_w_in = dot_to("rf,rd->fd", d_hidden, normed_low)
    ff_quarter = ff_half // 2
    d_w_ffo = d_w_ffo.astype(bf16)
    ffo_sums = sum_rows(
        *core_sum(
            d_w_ffo[:ff_half], d_w_ffo[ff_half : ff_half + ff_quarter], d_w_ffo[ff_half + ff_quarter :], core
        )
    )
    d_normed = d_second + dot_to("rf,df->rd", d_hidden, w_in_all)
    d_mid, unit1 = norm_back(d_normed, norm1_gain, centred1, inverse1)
    d_norm1_gain = jnp.sum(d_normed * unit1, axis=0)
    d_norm1_bias = jnp.sum(d_normed, axis=0)
    d_attn = d_mid.astype(bf16)
    d_w_out = dot_to("re,rd->ed", attended_flat, d_attn)
    d_attended = dot_to("rd,ed->re", d_attn, w_out_all).astype(bf16).reshape(attended.shape)


    shared = jnp.concatenate([d_norm1_gain, d_norm1_bias, d_norm2_gain, d_norm2_bias, d_b_ffo])
    shared = shared.reshape(-1, width)
    bias_far = ordered(core, d_b_in[ff_half : ff_half + ff_quarter], d_b_in[ff_half + ff_quarter :], 0)
    d_w_in, d_w_out = d_w_in.astype(bf16), d_w_out.astype(bf16)
    heads_width = width // 2
    rest = [
        padded(jnp.concatenate(
            [d_w_out[heads_width * at : heads_width * (at + 1)], shared.astype(bf16), bias.reshape(-1, width).astype(bf16)]
        ))
        for at, bias in enumerate((d_b_in[:ff_half], bias_far))
    ]
    in_sums = sum_rows(
        *core_sum(
            d_w_in[:ff_half], d_w_in[ff_half : ff_half + ff_quarter], d_w_in[ff_half + ff_quarter :], core
        )
    )
    rest_sums = sum_rows(
        *core_sum(rest[0], piece_of(rest[1], core, 2), piece_of(rest[1], 1 - core, 2), core)
    )

    embed_rows = jnp.transpose(embed_all, (1, 0, 2))
    embed_rows = jnp.concatenate([embed_rows, embed_rows], axis=-1)
    d_query, dk_own, dv_own, dk_ext, dv_ext, small, diag = attend_back(
        full, queries, key_own, value_own, key_ext, value_ext, lanes, attended, d_attended,
        (weight_own, weight_ext), embed_rows, content_all[:, :, None], diagonals.shape[-1],
    )
    aligned = []
    begin = 0
    for block in (rows, rows, mem_rows):
        piece = diag[:, :, begin : begin + block + rows]
        begin += block + rows
        aligned.append(sum(jnp.roll(piece[:, step], -step, axis=-1) for step in range(piece.shape[1])))
    d_rel = jnp.einsum("hl,rl->hr", jnp.concatenate(aligned, -1), hot, precision=highest) * SCALE
    odd = (jnp.arange(heads) % 2)[:, None, None]
    small = jnp.where(odd == 0, small[:, :, :HDIM], small[:, :, HDIM:]) * SCALE
    d_content_bias = small[:, 4]
    d_embed = [small[:, c] + small[:, 2 + c] * seg_all for c in range(2)]
    d_seg_bias = small[:, 2] * embed_all[0] + small[:, 3] * embed_all[1]

    pair_flat = pair.reshape(flat_rows, width)
    d_query_flat = d_query.reshape(flat_rows, width)
    d_wq = dot_to("re,rd->ed", d_query_flat, pair_flat)
    d_wk = dot_to("sej,sjd->ed", dk_own, content) + dot_to("sej,sjd->ed", dk_ext, ext_rows)
    d_wv = dot_to("sej,sjd->ed", dv_own, content) + dot_to("sej,sjd->ed", dv_ext, ext_rows)
    head_small = jnp.concatenate(
        [d_content_bias, d_seg_bias, d_embed[0], d_embed[1], d_rel], axis=1
    ).reshape(2, -1)
    small_size = head_small.shape[1]
    head_small = jnp.pad(head_small, ((0, 0), (0, -small_size % width))).reshape(2, -1, width)
    proj = padded(
        jnp.concatenate(
            [member.astype(bf16).reshape(2, heads_width, width) for member in (d_wq, d_wk, d_wv)]
            + [head_small.astype(bf16)],
            axis=1,
        )
    )
    proj_sums = sum_rows(
        *core_sum(proj[0], piece_of(proj[1], core, 2), piece_of(proj[1], 1 - core, 2), core)
    )

    def back_keys(dk, dv):
        def part(d_rows, weight):
            return dot_to("sej,de->sjd", d_rows, weight)

        return part(dk, wk) + part(dv, wv)

    d_ext = back_keys(dk_ext, dv_ext).astype(bf16)
    mem_mine = jnp.where(half == 0, d_ext[:, rows : rows + mem_half], d_ext[:, rows + mem_half :])
    mem_away = jnp.where(half == 0, d_ext[:, rows + mem_half :], d_ext[:, rows : rows + mem_half])
    arrived = other_of(jnp.concatenate([d_ext[:, :rows], mem_away], axis=1)).astype(f32)
    d_pair = (
        d_mid + dot_to("re,de->rd", d_query_flat, wq)
    ).reshape(slots, 2, rows, width)
    d_content = d_pair[:, 0] + back_keys(dk_own, dv_own) + arrived[:, :rows]
    d_memory = mem_mine.astype(f32) + arrived[:, rows:]

    vectors = rest_sums[heads_width : heads_width + 5].astype(f32)
    sum_b_in = rest_sums[heads_width + 5 :][: ff_half // width].astype(f32).reshape(-1)
    per_head_sums = proj_sums[3 * heads_width :].reshape(-1)[:small_size].astype(f32)
    per_head_sums = per_head_sums.reshape(heads_half, 4 * HDIM + NREL)
    d_small = [per_head_sums[:, HDIM * c : HDIM * (c + 1)] for c in range(4)]
    blocks = [proj_sums[heads_width * c : heads_width * (c + 1)].astype(f32).T for c in range(3)]
    return (
        outputs[:, 0][None],
        outputs[:, 1][None],
        d_content.astype(bf16)[None],
        d_pair[:, 1].astype(bf16)[None],
        d_memory.astype(bf16)[None],
        blocks[0],
        blocks[1],
        blocks[2],
        rest_sums[:heads_width].astype(f32),
        d_small[0],
        d_small[1],
        jnp.stack([d_small[2], d_small[3]]),
        per_head_sums[:, 4 * HDIM :],
        vectors[0],
        vectors[1],
        in_sums.astype(f32).T,
        sum_b_in,
        ffo_sums.astype(f32),
        vectors[4],
        vectors[2],
        vectors[3],
    )


def solution(mesh):
    rows = P("dp", None, "tensor", None)
    columns = P(None, "tensor")
    lead = P("tensor", None)
    group = P("dp", None, None)
    return jax.shard_map(
        per_device,
        mesh=mesh,
        in_specs=(
            rows, rows, rows, rows, rows, columns, columns, columns, lead, lead, lead,
            P(None, "tensor", None), lead, P(), P(), columns, P("tensor"), lead, P(), P(), P(),
            P("dp", None), group, group, group, group,
        ),
        out_specs=(
            rows, rows, rows, rows, rows, columns, columns, columns, lead, lead, lead,
            P(None, "tensor", None), lead, P(), P(), columns, P("tensor"), lead, P(), P(), P(),
        ),
        check_vma=False,
    )
```

```python
import jax
import jax.numpy as jnp
from jax import lax
from jax.experimental import pallas as pl
from jax.experimental.pallas import tpu as pltpu
from jax.sharding import PartitionSpec as P


HDIM = 64
NREL = 32
epsilon = 1e-05
masked_score = -1e30
target_floor = 48
distance_steps = (1, 2, 3, 4, 5, 6, 7, 8, 12, 16, 24, 32, 64, 128, 256)
highest = lax.Precision.HIGHEST
f32 = jnp.float32
bf16 = jnp.bfloat16
LANES = 128
ORDERS = 16
SCALE = HDIM ** (-0.5)


def bucket_of(distance):
    magnitude = jnp.abs(distance)
    counted = jnp.zeros(distance.shape, jnp.int32)
    for threshold in distance_steps:
        counted = counted + (magnitude >= threshold).astype(jnp.int32)
    return counted + NREL // 2 * (distance > 0).astype(jnp.int32)


def diagonal_buckets(half, rows, mem_rows):
    pieces = []
    for width, off in (
        (rows, 0),
        (rows, jnp.where(half == 0, -rows, rows)),
        (mem_rows, rows * half + mem_rows),
    ):
        length = width + rows
        lane = jnp.arange(length, dtype=jnp.int32)
        pieces.append(off + jnp.where(lane < width, -lane, length - lane))
    return bucket_of(jnp.concatenate(pieces))


def mask_lanes(bucket, doc_len, perm_rank, seg_ids, mem_seg):
    slot_rows = perm_rank.shape[0]
    mem_rows = mem_seg.shape[0]
    docs = doc_len.shape[0]
    positions = jnp.arange(slot_rows, dtype=jnp.int32)
    document = positions // bucket
    within = positions - document * bucket
    doc_index = jnp.arange(docs, dtype=jnp.int32)
    doc_length = jnp.sum(
        jnp.where(document[:, None] == doc_index[None, :], doc_len[None, :], 0), axis=1, dtype=jnp.int32
    )
    absent = within >= doc_length
    order = jnp.where(within < 2, 0, jnp.maximum(perm_rank - target_floor, 0))
    lane = jnp.arange(HDIM, dtype=jnp.int32)[None, :]
    slot_order = lane - 6
    slot_doc = lane - 6 - ORDERS
    in_order = (slot_order >= 0) & (slot_order < ORDERS)
    in_doc = (slot_doc >= 0) & (slot_doc < docs)
    is_absent = lane == 6 + ORDERS + docs
    one = (lane == 4) | (lane == 5)
    hide_doc = in_doc & (slot_doc != document[:, None])
    hide_content = in_order & (slot_order > order[:, None])
    hide_query = in_order & (slot_order >= order[:, None]) & (slot_order > 0)

    def query_side(hide):
        return jnp.where(one, 1.0, jnp.where(hide | hide_doc | is_absent, masked_score, 0.0))

    query_lanes = jnp.stack([query_side(hide_content), query_side(hide_query)])
    seg_lane = (lane == 2) | (lane == 3)
    ones_lane = lane < 2

    def key_side(segment, extra):
        return jnp.where(ones_lane, 1.0, jnp.where(seg_lane, segment[:, None].astype(f32), extra))

    token_hot = (
        (in_order & (slot_order == order[:, None]))
        | (in_doc & (slot_doc == document[:, None]))
        | (is_absent & absent[:, None])
    )
    key_lanes = key_side(seg_ids, token_hot.astype(f32))
    mem_lanes = key_side(mem_seg, jnp.zeros((mem_rows, HDIM), f32))

    def both(values_in):
        return jnp.concatenate([values_in, values_in], axis=-1).astype(bf16)

    return both(query_lanes), both(key_lanes), both(mem_lanes)


def split_pair(values_in):
    high = values_in.astype(bf16)
    return high, (values_in - high.astype(f32)).astype(bf16)


def head_tables(content_bias, seg_bias, seg_embed):
    heads = content_bias.shape[0]
    parity = (jnp.arange(heads) % 2)[:, None, None]
    row = jnp.arange(LANES)[None, :, None]
    lane = jnp.arange(LANES)[None, None, :]
    own_row = (row // HDIM) == parity
    spare = (lane // HDIM) != parity
    column = lane % HDIM

    def spread(vectors, lanes):
        tall = jnp.concatenate([vectors, vectors], axis=1)[:, :, None]
        keep = own_row & spare & ((column == lanes[0]) | (column == lanes[1]))
        parts = split_pair(tall)
        return jnp.concatenate([jnp.where(keep, part, jnp.zeros((), bf16)) for part in parts], axis=1)

    first, second = seg_embed[0], seg_embed[1]
    same_seg_one = spread(first, (0, 1)) + spread(second - first, (2, 3))
    same_seg_zero = spread(second, (0, 1)) + spread(first - second, (2, 3))
    seg_table = jnp.concatenate([same_seg_one, same_seg_zero], axis=2)
    key_table = spread(content_bias * SCALE, (4, 5))
    dots = [jnp.sum(seg_bias * part, axis=-1)[:, None] * SCALE for part in (first, second)]
    column = column[:, 0]
    spare = spare[:, 0]

    def const_row(start, slope):
        return jnp.where(spare & (column < 2), start, jnp.where(spare & (column >= 2) & (column < 4), slope, 0.0))

    seg_const = jnp.stack(
        [const_row(dots[0], dots[1] - dots[0]), const_row(dots[1], dots[0] - dots[1])], axis=1
    )
    return seg_table, seg_const, key_table


def nt(left, right):
    return lax.dot_general(left, right, (((1,), (1,)), ((), ())), preferred_element_type=f32)


def nn(left, right):
    return lax.dot_general(left, right, (((1,), (0,)), ((), ())), preferred_element_type=f32)


def tn(left, right):
    return lax.dot_general(left, right, (((0,), (0,)), ((), ())), preferred_element_type=f32)


def lane_of(shape):
    return lax.broadcasted_iota(jnp.int32, shape, len(shape) - 1)


def high_low(values_in, lane):
    high = values_in.astype(bf16).astype(f32)
    return jnp.where(lane % 2 == 0, high, values_in - high)


def attend_kernel(
    full_ref, q_ref, ko_ref, vo_ref, ke_ref, ve_ref, qm_ref, kmo_ref, kme_ref, seg_ref,
    st_ref, sc_ref, kt_ref, diag_ref,
    a_ref, po_ref, pe_ref,
    bo_ref, be_ref,
):
    slot = pl.program_id(1)
    rows = q_ref.shape[2]
    mem_rows = ke_ref.shape[1] - rows

    @pl.when(slot == 0)
    def _():
        for head in range(2):
            start = 0
            for ref, at, width in ((bo_ref, 0, rows), (be_ref, 0, rows), (be_ref, rows, mem_rows)):
                length = width + rows
                line = jnp.broadcast_to(diag_ref[head, :, start : start + length], (rows, length))
                skew = pltpu.roll(line, 0, 1, stride=1, stride_axis=0)
                ref[head, :, at : at + width] = skew[:, :width] * SCALE
                start += length

    lane = lane_of((rows, LANES))
    eye = lax.broadcasted_iota(jnp.int32, (rows, rows), 0) == lax.broadcasted_iota(jnp.int32, (rows, rows), 1)

    def keys_of(k_ref, km_ref, head):
        key_rows = k_ref[0]
        key_lane = lane_of(key_rows.shape)
        shift = nn(jnp.concatenate([key_rows, key_rows], axis=1), kt_ref[head])
        spare = high_low(shift, key_lane) + km_ref[0].astype(f32)
        return jnp.where(key_lane // HDIM == head, key_rows.astype(f32), spare).astype(bf16)

    def run(full):
        keys = [
            (keys_of(ko_ref, kmo_ref, head), keys_of(ke_ref, kme_ref, head) if full else None)
            for head in range(2)
        ]
        for stream in range(2):
            outs = []
            for head in range(2):
                own = lane // HDIM == head
                scaled = q_ref[0, stream] * jnp.asarray(SCALE, bf16)
                table = nn(jnp.concatenate([scaled, scaled], axis=1), st_ref[head])
                seg = jnp.where(
                    seg_ref[0] > 0,
                    table[:, :LANES] + sc_ref[head, 0:1],
                    table[:, LANES:] + sc_ref[head, 1:2],
                )
                spare = high_low(seg, lane) + qm_ref[0, stream].astype(f32)
                queries = jnp.where(own, scaled.astype(f32), spare).astype(bf16)
                key_own, key_ext = keys[head]
                score_own = nt(queries, key_own)
                if stream == 0:
                    plain = own | (lane % HDIM < 6)
                    product = jnp.where(plain, queries.astype(f32) * key_own.astype(f32), 0.0)
                    self_score = jnp.sum(product, axis=1, keepdims=True)
                else:
                    self_score = masked_score
                score_own = jnp.where(eye, self_score, score_own) + bo_ref[head]
                top = jnp.max(score_own, axis=1, keepdims=True)
                if full:
                    score_ext = nt(queries, key_ext) + be_ref[head]
                    top = jnp.maximum(top, jnp.max(score_ext, axis=1, keepdims=True))
                part_own = jnp.exp(score_own - top)
                total = jnp.sum(part_own, axis=1, keepdims=True)
                if full:
                    part_ext = jnp.exp(score_ext - top)
                    total = total + jnp.sum(part_ext, axis=1, keepdims=True)
                inverse = 1.0 / total
                weight_own = (part_own * inverse).astype(bf16)
                po_ref[0, stream, head] = weight_own
                out = nn(weight_own, vo_ref[0])
                if full:
                    weight_ext = (part_ext * inverse).astype(bf16)
                    pe_ref[0, stream, head] = weight_ext
                    out = out + nn(weight_ext, ve_ref[0])
                outs.append(out)
            a_ref[0, stream] = jnp.where(lane < HDIM, outs[0], outs[1]).astype(bf16)

    is_full = full_ref[slot] > 0

    @pl.when(is_full)
    def _():
        run(True)

    @pl.when(jnp.logical_not(is_full))
    def _():
        run(False)


def specs_of(rows, ext):
    by_pair = pl.BlockSpec((1, 2, rows, LANES), lambda p, s, *_: (s, 0, 0, p))
    own = pl.BlockSpec((1, rows, LANES), lambda p, s, *_: (s, 0, p))
    far = pl.BlockSpec((1, ext, LANES), lambda p, s, *_: (s, 0, p))
    own_lanes = pl.BlockSpec((1, rows, LANES), lambda p, s, *_: (s, 0, 0))
    far_lanes = pl.BlockSpec((1, ext, LANES), lambda p, s, *_: (s, 0, 0))
    query_lanes = pl.BlockSpec((1, 2, rows, LANES), lambda p, s, *_: (s, 0, 0, 0))
    weight_own = pl.BlockSpec((1, 2, 2, rows, rows), lambda p, s, *_: (s, 0, p, 0, 0))
    weight_far = pl.BlockSpec((1, 2, 2, rows, ext), lambda p, s, *_: (s, 0, p, 0, 0))
    return by_pair, own, far, own_lanes, far_lanes, query_lanes, weight_own, weight_far


def per_head(*shape):
    return pl.BlockSpec((2,) + shape, lambda p, s, *_: (p,) + (0,) * len(shape))


def attend(full, queries, key_own, value_own, key_ext, value_ext, lanes, tables, diagonals):
    slots, streams, rows, width = queries.shape
    ext = key_ext.shape[1]
    heads = width // HDIM
    query_lanes, own_lanes, ext_lanes, seg_rows = lanes
    seg_table, seg_const, key_table = tables
    pair, own, far, own_l, far_l, query_l, w_own, w_far = specs_of(rows, ext)
    return pl.pallas_call(
        attend_kernel,
        grid_spec=pltpu.PrefetchScalarGridSpec(
            num_scalar_prefetch=1,
            grid=(heads // 2, slots),
            in_specs=[
                pair, own, own, far, far, query_l, own_l, far_l, own_l,
                per_head(2 * LANES, 2 * LANES), per_head(2, LANES), per_head(2 * LANES, LANES),
                per_head(1, diagonals.shape[-1]),
            ],
            out_specs=[pair, w_own, w_far],
            scratch_shapes=[pltpu.VMEM((2, rows, rows), f32), pltpu.VMEM((2, rows, ext), f32)],
        ),
        out_shape=[
            jax.ShapeDtypeStruct(queries.shape, bf16),
            jax.ShapeDtypeStruct((slots, streams, heads, rows, rows), bf16),
            jax.ShapeDtypeStruct((slots, streams, heads, rows, ext), bf16),
        ],
        name="attend",
    )(full, queries, key_own, value_own, key_ext, value_ext, query_lanes, own_lanes, ext_lanes, seg_rows,
      seg_table, seg_const, key_table, diagonals)


def attend_back_kernel(
    full_ref, q_ref, ko_ref, vo_ref, ke_ref, ve_ref, kmo_ref, kme_ref, seg_ref,
    a_ref, da_ref, po_ref, pe_ref, emb_ref, cb_ref,
    dq_ref, dko_ref, dvo_ref, dke_ref, dve_ref, small_ref, diag_ref,
    bo_ref, be_ref,
):
    slot = pl.program_id(1)
    rows = q_ref.shape[2]
    ext = ke_ref.shape[1]
    lane = lane_of((rows, LANES))

    @pl.when(slot == 0)
    def _():
        bo_ref[...] = jnp.zeros_like(bo_ref)
        be_ref[...] = jnp.zeros_like(be_ref)
        small_ref[...] = jnp.zeros_like(small_ref)

    def keys_of(k_ref, km_ref, head):
        key_lane = lane_of(k_ref.shape[1:])
        return jnp.where(key_lane // HDIM == head, k_ref[0], km_ref[0])

    def run(full):
        parts = [(ko_ref, vo_ref, kmo_ref, po_ref, bo_ref, dko_ref, dvo_ref)]
        if full:
            parts.append((ke_ref, ve_ref, kme_ref, pe_ref, be_ref, dke_ref, dve_ref))
        d_queries = [[None, None], [None, None]]
        for head in range(2):
            own = lane // HDIM == head
            base = HDIM * (1 - head)
            key_sets = [keys_of(k_ref, km_ref, head) for k_ref, _, km_ref, *_ in parts]
            d_keys = [0.0] * len(parts)
            d_values = [0.0] * len(parts)
            totals = [jnp.zeros((1, LANES), f32)] * 5
            for stream in range(2):
                queries = q_ref[0, stream]
                flat = jnp.where(
                    own,
                    queries.astype(f32) * SCALE,
                    jnp.where(lane % HDIM == 4, 1.0, 0.0),
                ).astype(bf16)
                cot = jnp.where(own, da_ref[0, stream].astype(f32), 0.0)
                inner = jnp.sum(cot * a_ref[0, stream].astype(f32), axis=1, keepdims=True)
                cot = cot.astype(bf16)
                d_rows = 0.0
                for at, (k_ref, v_ref, km_ref, p_ref, b_ref, dk_ref, dv_ref) in enumerate(parts):
                    weights = p_ref[0, stream, head]
                    d_scores = weights.astype(f32) * (nt(cot, v_ref[0]) - inner)
                    b_ref[head] += d_scores
                    d_scores = d_scores.astype(bf16)
                    d_rows = d_rows + nn(d_scores, key_sets[at])
                    d_keys[at] = d_keys[at] + tn(flat, d_scores)
                    d_values[at] = d_values[at] + tn(cot, weights)
                every = d_rows[:, base : base + 1]
                ones = d_rows[:, base + 2 : base + 3]
                same = jnp.where(seg_ref[0] > 0, ones, every - ones)
                other = every - same
                d_queries[stream][head] = SCALE * (
                    d_rows + other * emb_ref[head, 0:1] + same * emb_ref[head, 1:2]
                )
                wide = queries.astype(f32)
                for row, member in enumerate((other * wide, same * wide, other, same, d_rows)):
                    totals[row] = totals[row] + jnp.sum(member, axis=0, keepdims=True)
            for row in range(5):
                small_ref[head, row : row + 1] += totals[row]
            for at, (k_ref, v_ref, km_ref, p_ref, b_ref, dk_ref, dv_ref) in enumerate(parts):
                column = d_keys[at][base + 4 : base + 5]
                mine = slice(HDIM * head, HDIM * head + HDIM)
                dk_ref[0, mine] = (d_keys[at][mine] + cb_ref[head] * SCALE * column).astype(bf16)
                dv_ref[0, mine] = d_values[at][mine].astype(bf16)
        for stream in range(2):
            dq_ref[0, stream] = jnp.where(lane < HDIM, d_queries[stream][0], d_queries[stream][1]).astype(bf16)

    is_full = full_ref[slot] > 0

    @pl.when(is_full)
    def _():
        run(True)

    @pl.when(jnp.logical_not(is_full))
    def _():
        run(False)
        dke_ref[...] = jnp.zeros_like(dke_ref)
        dve_ref[...] = jnp.zeros_like(dve_ref)

    @pl.when(slot == pl.num_programs(1) - 1)
    def _():
        for head in range(2):
            start = 0
            for ref, at, width in ((bo_ref, 0, rows), (be_ref, 0, rows), (be_ref, rows, ext - rows)):
                length = width + rows
                block = jnp.concatenate([ref[head, :, at : at + width], jnp.zeros((rows, rows), f32)], axis=1)
                step = rows // 2
                while step >= 8:
                    block = block[:step] + pltpu.roll(block[step:], length - step, 1)
                    step //= 2
                while step >= 1:
                    block = block + pltpu.roll(pltpu.roll(block, length - step, 1), 8 - step, 0)
                    step //= 2
                diag_ref[head, :, start : start + length] = block[:1]
                start += length


def attend_back(
    full, queries, key_own, value_own, key_ext, value_ext, lanes, attended, d_attended, weights,
    seg_rows_embed, bias_columns, diag_length,
):
    slots, _, rows, width = queries.shape
    ext = key_ext.shape[1]
    heads = width // HDIM
    _, own_lanes, ext_lanes, seg_rows = lanes
    pair, own, far, own_l, far_l, _, w_own, w_far = specs_of(rows, ext)
    tall_own = pl.BlockSpec((1, LANES, rows), lambda p, s, *_: (s, p, 0))
    tall_ext = pl.BlockSpec((1, LANES, ext), lambda p, s, *_: (s, p, 0))
    return pl.pallas_call(
        attend_back_kernel,
        grid_spec=pltpu.PrefetchScalarGridSpec(
            num_scalar_prefetch=1,
            grid=(heads // 2, slots),
            in_specs=[
                pair, own, own, far, far, own_l, far_l, own_l, pair, pair, w_own, w_far,
                per_head(2, LANES), per_head(HDIM, 1),
            ],
            out_specs=[pair, tall_own, tall_own, tall_ext, tall_ext, per_head(8, LANES), per_head(1, diag_length)],
            scratch_shapes=[pltpu.VMEM((2, rows, rows), f32), pltpu.VMEM((2, rows, ext), f32)],
        ),
        out_shape=[
            jax.ShapeDtypeStruct(queries.shape, bf16),
            jax.ShapeDtypeStruct((slots, width, rows), bf16),
            jax.ShapeDtypeStruct((slots, width, rows), bf16),
            jax.ShapeDtypeStruct((slots, width, ext), bf16),
            jax.ShapeDtypeStruct((slots, width, ext), bf16),
            jax.ShapeDtypeStruct((heads, 8, LANES), f32),
            jax.ShapeDtypeStruct((heads, 1, diag_length), f32),
        ],
        name="attend_back",
    )(full, queries, key_own, value_own, key_ext, value_ext, own_lanes, ext_lanes, seg_rows,
      attended, d_attended, weights[0], weights[1], seg_rows_embed, bias_columns)


def other_of(values_in):
    size = lax.axis_size("tensor")
    return lax.ppermute(values_in, "tensor", [(i, (i + 1) % size) for i in range(size)])


def across(values_in, step):
    return lax.ppermute(values_in, "dp", [(i, i ^ step) for i in range(lax.axis_size("dp"))])


def ordered(bit, mine, other, axis):
    first = jnp.where(bit == 0, mine, other)
    second = jnp.where(bit == 0, other, mine)
    return jnp.concatenate([first, second], axis=axis)


def piece_of(values_in, at, count, axis=0):
    size = values_in.shape[axis] // count
    return lax.dynamic_slice_in_dim(values_in, at * size, size, axis)


def fetch_half(values_in, core, axis):
    piece = piece_of(values_in, core, 2, axis)
    near = other_of(piece)
    return near, across(near, 1)


def dp_steps():
    steps = []
    step = 2
    while step < lax.axis_size("dp"):
        steps.append(step)
        step *= 2
    return steps


def add_low(first, second):
    return (first.astype(f32) + second.astype(f32)).astype(bf16)


def sum_rows(mine, away, axis):
    dp = lax.axis_index("dp")
    arrived = other_of(away)
    total = add_low(mine, arrived)
    for step in dp_steps():
        bit = (dp // step) % 2
        total = add_low(piece_of(total, bit, 2), across(piece_of(total, 1 - bit, 2), step))
    for step in reversed(dp_steps()):
        total = ordered((dp // step) % 2, total, across(total, step), 0)
    return ordered(dp % 2, total, across(total, 1), axis)


def core_sum(own_half, near, far, core, axis):
    sent = jnp.concatenate([piece_of(own_half, 1 - core, 2, axis), far], axis=axis)
    kept = jnp.concatenate([piece_of(own_half, core, 2, axis), near], axis=axis)
    total = add_low(kept, across(sent, 1))
    size = near.shape[axis]
    return lax.slice_in_dim(total, 0, size, axis=axis), lax.slice_in_dim(total, size, 2 * size, axis=axis)


def padded(values_in):
    rows = values_in.shape[-2]
    block = 16 * lax.axis_size("dp")
    return jnp.pad(values_in, [(0, 0)] * (values_in.ndim - 2) + [(0, -rows % block), (0, 0)])


def after(values_in, *others):
    return lax.optimization_barrier((values_in,) + others)[0]


def norm_parts(values_in):
    centred = values_in - jnp.mean(values_in, axis=-1, keepdims=True)
    spread = jnp.mean(centred * centred, axis=-1, keepdims=True)
    return centred, lax.rsqrt(spread + epsilon)


def norm_back(cotangent, gain, centred, inverse):
    unit = centred * inverse
    scaled = cotangent * gain
    first = jnp.mean(scaled, axis=-1, keepdims=True)
    second = jnp.mean(scaled * unit, axis=-1, keepdims=True)
    return inverse * (scaled - first - unit * second), unit


def gelu_pair(values_in):
    rate = 0.7978845608028654
    square = values_in * values_in
    bent = jnp.tanh(rate * values_in * (1.0 + 0.044715 * square))
    half = 0.5 * (1.0 + bent)
    slope = half + 0.5 * values_in * (1.0 - bent * bent) * rate * (1.0 + 3 * 0.044715 * square)
    return values_in * half, slope


def dot_to(equation, left, right):
    return jnp.einsum(equation, left, right, preferred_element_type=f32)


def per_device(
    h_in, g_in, mem_in, d_h_out, d_g_out, w_query, w_key, w_value, w_out, content_bias, seg_bias,
    seg_embed, rel_table, norm1_gain, norm1_bias, w_in, b_in, w_ffo, b_ffo, norm2_gain, norm2_bias,
    bucket_len, doc_len, seg_ids, mem_seg, perm_rank,
):
    half = lax.axis_index("tensor")
    content, stream, memory = h_in[0], g_in[0], mem_in[0]
    slots, rows, width = content.shape
    mem_half = memory.shape[1]
    slot_rows = perm_rank.shape[2]
    mem_rows = mem_seg.shape[2]
    heads_half = w_query.shape[1] // HDIM

    core = lax.axis_index("dp") % 2

    proj_own = jnp.stack([w_query, w_key, w_value])
    proj_far = ordered(core, *fetch_half(proj_own, core, 1), 1)
    wq, wk, wv = [jnp.concatenate([proj_own[c], proj_far[c]], axis=1) for c in range(3)]
    other_rows = other_of(jnp.concatenate([content, memory], axis=1))
    w_out_far = fetch_half(after(w_out, other_rows), core, 0)
    w_out_all = jnp.concatenate([w_out, ordered(core, *w_out_far, 0)], axis=0)
    table_half = jnp.concatenate(
        [content_bias, seg_bias, seg_embed[0], seg_embed[1], rel_table], axis=1
    )
    small_half = jnp.concatenate([table_half.reshape(-1), b_in])
    small_other = other_of(small_half)
    cut = table_half.size
    tables = jnp.concatenate([table_half, small_other[:cut].reshape(table_half.shape)], axis=0)
    content_all, seg_all = tables[:, :HDIM], tables[:, HDIM : 2 * HDIM]
    embed_all = jnp.stack([tables[:, 2 * HDIM : 3 * HDIM], tables[:, 3 * HDIM : 4 * HDIM]])
    rel_all = tables[:, 4 * HDIM :]
    heads = rel_all.shape[0]
    ff_half = w_in.shape[1]
    w_in_near, w_in_far = fetch_half(after(w_in, other_rows), core, 1)
    w_in_all = jnp.concatenate([w_in, w_in_near, w_in_far], axis=1)
    w_ffo_near, w_ffo_far = fetch_half(after(w_ffo, w_out_far[0]), core, 0)
    w_ffo_all = jnp.concatenate([w_ffo, w_ffo_near, w_ffo_far], axis=0)
    bias_other = small_other[cut:]
    hidden_bias = jnp.concatenate(
        [b_in, piece_of(bias_other, core, 2), piece_of(bias_other, 1 - core, 2)]
    )

    full = (bucket_len[0] == slot_rows).astype(jnp.int32)
    query_lanes, key_lanes, mem_lanes = jax.vmap(mask_lanes)(
        bucket_len[0], doc_len[0], perm_rank[0], seg_ids[0], mem_seg[0]
    )
    start = half * rows
    far = slot_rows - rows - start

    def own_of(values_in, axis):
        return lax.dynamic_slice_in_dim(values_in, start, rows, axis)

    seg_rows = jnp.broadcast_to(
        own_of(seg_ids[0], 1).astype(f32)[:, :, None], (slots, rows, LANES)
    )
    lanes = (
        own_of(query_lanes, 2),
        own_of(key_lanes, 1),
        jnp.concatenate([lax.dynamic_slice_in_dim(key_lanes, far, rows, 1), mem_lanes], axis=1),
        seg_rows,
    )
    head_set = head_tables(content_all, seg_all, embed_all)
    buckets = diagonal_buckets(half, rows, mem_rows)
    hot = (buckets[None] == jnp.arange(NREL, dtype=jnp.int32)[:, None]).astype(f32)
    diagonals = jnp.dot(rel_all, hot, precision=highest)[:, None]

    pair = jnp.stack([content, stream], axis=1)

    def project(values_in, weight):
        return dot_to("sjd,de->sje", values_in, weight).astype(bf16)

    flat_pair = pair.reshape(slots, 2 * rows, width)
    queries = project(flat_pair, wq).reshape(slots, 2, rows, -1)
    ext_rows = jnp.concatenate(
        [other_rows[:, :rows], ordered(half, memory, other_rows[:, rows:], 1)], axis=1
    )
    key_own, value_own = project(content, wk), project(content, wv)
    key_ext, value_ext = project(ext_rows, wk), project(ext_rows, wv)

    attended, weight_own, weight_ext = attend(
        full, queries, key_own, value_own, key_ext, value_ext, lanes, head_set, diagonals
    )

    flat_rows = slots * 2 * rows
    attended_flat = attended.reshape(flat_rows, width)
    mid = pair.reshape(flat_rows, width).astype(f32) + dot_to("re,ed->rd", attended_flat, w_out_all)
    centred1, inverse1 = norm_parts(mid)
    normed = centred1 * inverse1 * norm1_gain + norm1_bias
    normed_low = normed.astype(bf16)
    hidden = dot_to("rd,df->rf", normed_low, w_in_all) + hidden_bias
    active, slope = gelu_pair(hidden)
    active = active.astype(bf16)
    second = normed + dot_to("rf,fd->rd", active, w_ffo_all) + b_ffo
    centred2, inverse2 = norm_parts(second)
    outputs = (centred2 * inverse2 * norm2_gain + norm2_bias).astype(bf16).reshape(pair.shape)

    cot = jnp.stack([d_h_out[0], d_g_out[0]], axis=1).reshape(flat_rows, width).astype(f32)
    d_second, unit2 = norm_back(cot, norm2_gain, centred2, inverse2)
    d_norm2_gain = jnp.sum(cot * unit2, axis=0)
    d_norm2_bias = jnp.sum(cot, axis=0)
    d_ffn = d_second.astype(bf16)
    d_b_ffo = jnp.sum(d_ffn.astype(f32), axis=0)
    d_hidden = (dot_to("rd,fd->rf", d_ffn, w_ffo_all) * slope).astype(bf16)
    d_b_in = jnp.sum(d_hidden.astype(f32), axis=0)
    ff_quarter = ff_half // 2
    d_w_in = dot_to("rd,rf->df", normed_low, d_hidden).astype(bf16)
    in_parts = core_sum(
        d_w_in[:, :ff_half],
        d_w_in[:, ff_half : ff_half + ff_quarter],
        d_w_in[:, ff_half + ff_quarter :],
        core,
        1,
    )
    in_sums = sum_rows(*in_parts, 1)
    d_w_ffo = dot_to("rf,rd->fd", active, d_ffn).astype(bf16)
    d_normed = d_second + dot_to("rf,df->rd", d_hidden, w_in_all)
    d_mid, unit1 = norm_back(d_normed, norm1_gain, centred1, inverse1)
    d_norm1_gain = jnp.sum(d_normed * unit1, axis=0)
    d_norm1_bias = jnp.sum(d_normed, axis=0)
    d_attn = d_mid.astype(bf16)
    d_w_out = dot_to("re,rd->ed", attended_flat, d_attn)
    d_attended = dot_to("rd,ed->re", d_attn, w_out_all).astype(bf16).reshape(attended.shape)


    shared = jnp.concatenate([d_norm1_gain, d_norm1_bias, d_norm2_gain, d_norm2_bias, d_b_ffo])
    shared = shared.reshape(-1, width)
    d_w_out = d_w_out.astype(bf16)
    heads_width = width // 2
    far_start = ff_half + ff_quarter
    bias_far = ordered(core, d_b_in[ff_half:far_start], d_b_in[far_start:], 0)
    own_rest, far_rest = [
        padded(jnp.concatenate(
            [d_w_out[heads_width * at : heads_width * (at + 1)], shared.astype(bf16), bias.reshape(-1, width).astype(bf16)]
        ))
        for at, bias in enumerate((d_b_in[:ff_half], bias_far))
    ]
    rest_size = own_rest.shape[0] // 2
    stacked = jnp.concatenate(
        [piece_of(d_w_ffo[:ff_half], core, 2), piece_of(own_rest, core, 2),
         d_w_ffo[ff_half:far_start], piece_of(far_rest, core, 2)]
    )
    outgoing = jnp.concatenate(
        [piece_of(d_w_ffo[:ff_half], 1 - core, 2), piece_of(own_rest, 1 - core, 2),
         d_w_ffo[far_start:], piece_of(far_rest, 1 - core, 2)]
    )
    chip_sum = add_low(stacked, across(outgoing, 1))
    part_size = ff_quarter + rest_size
    out_sums = sum_rows(chip_sum[:part_size], chip_sum[part_size:], 0)
    out_sums = out_sums.reshape(2, part_size, width)
    ffo_sums = out_sums[:, :ff_quarter].reshape(ff_half, width)
    rest_sums = out_sums[:, ff_quarter:].reshape(2 * rest_size, width)

    embed_rows = jnp.transpose(embed_all, (1, 0, 2))
    embed_rows = jnp.concatenate([embed_rows, embed_rows], axis=-1)
    d_attended = after(d_attended, chip_sum, *in_parts)
    d_query, dk_own, dv_own, dk_ext, dv_ext, small, diag = attend_back(
        full, queries, key_own, value_own, key_ext, value_ext, lanes, attended, d_attended,
        (weight_own, weight_ext), embed_rows, content_all[:, :, None], diagonals.shape[-1],
    )
    d_rel = jnp.einsum("hl,rl->hr", diag[:, 0], hot, precision=highest) * SCALE
    odd = (jnp.arange(heads) % 2)[:, None, None]
    small = jnp.where(odd == 0, small[:, :, :HDIM], small[:, :, HDIM:]) * SCALE
    d_content_bias = small[:, 4]
    d_embed = [small[:, c] + small[:, 2 + c] * seg_all for c in range(2)]
    d_seg_bias = small[:, 2] * embed_all[0] + small[:, 3] * embed_all[1]

    pair_flat = pair.reshape(flat_rows, width)
    d_query_flat = d_query.reshape(flat_rows, width)
    d_wq = dot_to("re,rd->ed", d_query_flat, pair_flat)
    d_wk = dot_to("sej,sjd->ed", dk_own, content) + dot_to("sej,sjd->ed", dk_ext, ext_rows)
    d_wv = dot_to("sej,sjd->ed", dv_own, content) + dot_to("sej,sjd->ed", dv_ext, ext_rows)
    head_small = jnp.concatenate(
        [d_content_bias, d_seg_bias, d_embed[0], d_embed[1], d_rel], axis=1
    ).reshape(2, -1)
    small_size = head_small.shape[1]
    head_small = jnp.pad(head_small, ((0, 0), (0, -small_size % width))).reshape(2, -1, width)
    own_proj, far_proj = [
        padded(
            jnp.concatenate(
                [member[heads_width * at : heads_width * (at + 1)].astype(bf16) for member in (d_wq, d_wk, d_wv)]
                + [head_small[at].astype(bf16)]
            )
        )
        for at in range(2)
    ]
    proj_parts = core_sum(own_proj, piece_of(far_proj, core, 2), piece_of(far_proj, 1 - core, 2), core, 0)
    proj_sums = sum_rows(*proj_parts, 0)

    def back_keys(dk, dv):
        def part(d_rows, weight):
            return dot_to("sej,de->sjd", d_rows, weight)

        return part(dk, wk) + part(dv, wv)

    d_ext = back_keys(dk_ext, dv_ext).astype(bf16)
    mem_mine = jnp.where(half == 0, d_ext[:, rows : rows + mem_half], d_ext[:, rows + mem_half :])
    mem_away = jnp.where(half == 0, d_ext[:, rows + mem_half :], d_ext[:, rows : rows + mem_half])
    arrived = other_of(jnp.concatenate([d_ext[:, :rows], mem_away], axis=1)).astype(f32)
    d_pair = (
        d_mid + dot_to("re,de->rd", d_query_flat, wq)
    ).reshape(slots, 2, rows, width)
    d_content = d_pair[:, 0] + back_keys(dk_own, dv_own) + arrived[:, :rows]
    d_memory = mem_mine.astype(f32) + arrived[:, rows:]

    vectors = rest_sums[heads_width : heads_width + 5].astype(f32)
    sum_b_in = rest_sums[heads_width + 5 :][: ff_half // width].astype(f32).reshape(-1)
    per_head_sums = proj_sums[3 * heads_width :].reshape(-1)[:small_size].astype(f32)
    per_head_sums = per_head_sums.reshape(heads_half, 4 * HDIM + NREL)
    d_small = [per_head_sums[:, HDIM * c : HDIM * (c + 1)] for c in range(4)]
    blocks = [proj_sums[heads_width * c : heads_width * (c + 1)].astype(f32).T for c in range(3)]
    return (
        outputs[:, 0][None],
        outputs[:, 1][None],
        d_content.astype(bf16)[None],
        d_pair[:, 1].astype(bf16)[None],
        d_memory.astype(bf16)[None],
        blocks[0],
        blocks[1],
        blocks[2],
        rest_sums[:heads_width].astype(f32),
        d_small[0],
        d_small[1],
        jnp.stack([d_small[2], d_small[3]]),
        per_head_sums[:, 4 * HDIM :],
        vectors[0],
        vectors[1],
        in_sums.astype(f32),
        sum_b_in,
        ffo_sums.astype(f32),
        vectors[4],
        vectors[2],
        vectors[3],
    )


def solution(mesh):
    rows = P("dp", None, "tensor", None)
    columns = P(None, "tensor")
    lead = P("tensor", None)
    group = P("dp", None, None)
    return jax.shard_map(
        per_device,
        mesh=mesh,
        in_specs=(
            rows, rows, rows, rows, rows, columns, columns, columns, lead, lead, lead,
            P(None, "tensor", None), lead, P(), P(), columns, P("tensor"), lead, P(), P(), P(),
            P("dp", None), group, group, group, group,
        ),
        out_specs=(
            rows, rows, rows, rows, rows, columns, columns, columns, lead, lead, lead,
            P(None, "tensor", None), lead, P(), P(), columns, P("tensor"), lead, P(), P(), P(),
        ),
        check_vma=False,
    )
```

```python
import jax
import jax.numpy as jnp
from jax import lax
from jax.experimental import pallas as pl
from jax.experimental.pallas import tpu as pltpu
from jax.sharding import Mesh, PartitionSpec as P


HDIM = 64
NREL = 32
epsilon = 1e-05
masked_score = -1e30
target_floor = 48
distance_steps = (1, 2, 3, 4, 5, 6, 7, 8, 12, 16, 24, 32, 64, 128, 256)
highest = lax.Precision.HIGHEST
f32 = jnp.float32
bf16 = jnp.bfloat16
LANES = 128
ORDERS = 16
SCALE = HDIM ** (-0.5)


def bucket_of(distance):
    magnitude = jnp.abs(distance)
    counted = jnp.zeros(distance.shape, jnp.int32)
    for threshold in distance_steps:
        counted = counted + (magnitude >= threshold).astype(jnp.int32)
    return counted + NREL // 2 * (distance > 0).astype(jnp.int32)


def diagonal_buckets(half, rows, mem_rows):
    pieces = []
    for width, off in (
        (rows, 0),
        (rows, jnp.where(half == 0, -rows, rows)),
        (mem_rows, rows * half + mem_rows),
    ):
        length = width + rows
        lane = jnp.arange(length, dtype=jnp.int32)
        pieces.append(off + jnp.where(lane < width, -lane, length - lane))
    return bucket_of(jnp.concatenate(pieces))


def mask_lanes(bucket, doc_len, perm_rank, seg_ids, mem_seg):
    slot_rows = perm_rank.shape[0]
    mem_rows = mem_seg.shape[0]
    docs = doc_len.shape[0]
    positions = jnp.arange(slot_rows, dtype=jnp.int32)
    document = positions // bucket
    within = positions - document * bucket
    doc_index = jnp.arange(docs, dtype=jnp.int32)
    doc_length = jnp.sum(
        jnp.where(document[:, None] == doc_index[None, :], doc_len[None, :], 0), axis=1, dtype=jnp.int32
    )
    absent = within >= doc_length
    order = jnp.where(within < 2, 0, jnp.maximum(perm_rank - target_floor, 0))
    lane = jnp.arange(HDIM, dtype=jnp.int32)[None, :]
    slot_order = lane - 6
    slot_doc = lane - 6 - ORDERS
    in_order = (slot_order >= 0) & (slot_order < ORDERS)
    in_doc = (slot_doc >= 0) & (slot_doc < docs)
    is_absent = lane == 6 + ORDERS + docs
    one = (lane == 4) | (lane == 5)
    hide_doc = in_doc & (slot_doc != document[:, None])
    hide_content = in_order & (slot_order > order[:, None])
    hide_query = in_order & (slot_order >= order[:, None]) & (slot_order > 0)

    def query_side(hide):
        return jnp.where(one, 1.0, jnp.where(hide | hide_doc | is_absent, masked_score, 0.0))

    query_lanes = jnp.stack([query_side(hide_content), query_side(hide_query)])
    seg_lane = (lane == 2) | (lane == 3)
    ones_lane = lane < 2

    def key_side(segment, extra):
        return jnp.where(ones_lane, 1.0, jnp.where(seg_lane, segment[:, None].astype(f32), extra))

    token_hot = (
        (in_order & (slot_order == order[:, None]))
        | (in_doc & (slot_doc == document[:, None]))
        | (is_absent & absent[:, None])
    )
    key_lanes = key_side(seg_ids, token_hot.astype(f32))
    mem_lanes = key_side(mem_seg, jnp.zeros((mem_rows, HDIM), f32))

    def both(values_in):
        return jnp.concatenate([values_in, values_in], axis=-1).astype(bf16)

    return both(query_lanes), both(key_lanes), both(mem_lanes)


def split_pair(values_in):
    high = values_in.astype(bf16)
    return high, (values_in - high.astype(f32)).astype(bf16)


def head_tables(content_bias, seg_bias, seg_embed):
    heads = content_bias.shape[0]
    parity = (jnp.arange(heads) % 2)[:, None, None]
    row = jnp.arange(LANES)[None, :, None]
    lane = jnp.arange(LANES)[None, None, :]
    own_row = (row // HDIM) == parity
    spare = (lane // HDIM) != parity
    column = lane % HDIM

    def spread(vectors, lanes):
        tall = jnp.concatenate([vectors, vectors], axis=1)[:, :, None]
        keep = own_row & spare & ((column == lanes[0]) | (column == lanes[1]))
        parts = split_pair(tall)
        return jnp.concatenate([jnp.where(keep, part, jnp.zeros((), bf16)) for part in parts], axis=1)

    first, second = seg_embed[0], seg_embed[1]
    same_seg_one = spread(first, (0, 1)) + spread(second - first, (2, 3))
    same_seg_zero = spread(second, (0, 1)) + spread(first - second, (2, 3))
    seg_table = jnp.concatenate([same_seg_one, same_seg_zero], axis=2)
    key_table = spread(content_bias * SCALE, (4, 5))
    dots = [jnp.sum(seg_bias * part, axis=-1)[:, None] * SCALE for part in (first, second)]
    column = column[:, 0]
    spare = spare[:, 0]

    def const_row(start, slope):
        return jnp.where(spare & (column < 2), start, jnp.where(spare & (column >= 2) & (column < 4), slope, 0.0))

    seg_const = jnp.stack(
        [const_row(dots[0], dots[1] - dots[0]), const_row(dots[1], dots[0] - dots[1])], axis=1
    )
    return seg_table, seg_const, key_table


def nt(left, right):
    return lax.dot_general(left, right, (((1,), (1,)), ((), ())), preferred_element_type=f32)


def nn(left, right):
    return lax.dot_general(left, right, (((1,), (0,)), ((), ())), preferred_element_type=f32)


def tn(left, right):
    return lax.dot_general(left, right, (((0,), (0,)), ((), ())), preferred_element_type=f32)


def lane_of(shape):
    return lax.broadcasted_iota(jnp.int32, shape, len(shape) - 1)


def high_low(values_in, lane):
    high = values_in.astype(bf16).astype(f32)
    return jnp.where(lane % 2 == 0, high, values_in - high)


def attend_kernel(
    full_ref, qc_ref, qg_ref, ko_ref, vo_ref, ke_ref, ve_ref, qm_ref, kmo_ref, kme_ref, seg_ref,
    st_ref, sc_ref, kt_ref, diag_ref,
    a_ref, po_ref, pe_ref,
    bo_ref, be_ref,
):
    slot = pl.program_id(1)
    rows = qc_ref.shape[1]
    mem_rows = ke_ref.shape[1] - rows

    @pl.when(slot == 0)
    def _():
        for head in range(2):
            start = 0
            for ref, at, width in ((bo_ref, 0, rows), (be_ref, 0, rows), (be_ref, rows, mem_rows)):
                length = width + rows
                line = jnp.broadcast_to(diag_ref[head, :, start : start + length], (rows, length))
                skew = pltpu.roll(line, 0, 1, stride=1, stride_axis=0)
                ref[head, :, at : at + width] = skew[:, :width] * SCALE
                start += length

    lane = lane_of((rows, LANES))
    eye = lax.broadcasted_iota(jnp.int32, (rows, rows), 0) == lax.broadcasted_iota(jnp.int32, (rows, rows), 1)

    def keys_of(k_ref, km_ref, head):
        key_rows = k_ref[0]
        key_lane = lane_of(key_rows.shape)
        shift = nn(jnp.concatenate([key_rows, key_rows], axis=1), kt_ref[head])
        spare = high_low(shift, key_lane) + km_ref[0].astype(f32)
        return jnp.where(key_lane // HDIM == head, key_rows.astype(f32), spare).astype(bf16)

    def run(full):
        keys = [
            (keys_of(ko_ref, kmo_ref, head), keys_of(ke_ref, kme_ref, head) if full else None)
            for head in range(2)
        ]
        for stream in range(2):
            outs = []
            for head in range(2):
                own = lane // HDIM == head
                scaled = (qc_ref, qg_ref)[stream][0] * jnp.asarray(SCALE, bf16)
                table = nn(jnp.concatenate([scaled, scaled], axis=1), st_ref[head])
                seg = jnp.where(
                    seg_ref[0] > 0,
                    table[:, :LANES] + sc_ref[head, 0:1],
                    table[:, LANES:] + sc_ref[head, 1:2],
                )
                spare = high_low(seg, lane) + qm_ref[0, stream].astype(f32)
                queries = jnp.where(own, scaled.astype(f32), spare).astype(bf16)
                key_own, key_ext = keys[head]
                score_own = nt(queries, key_own)
                if stream == 0:
                    plain = own | (lane % HDIM < 6)
                    product = jnp.where(plain, queries.astype(f32) * key_own.astype(f32), 0.0)
                    self_score = jnp.sum(product, axis=1, keepdims=True)
                else:
                    self_score = masked_score
                score_own = jnp.where(eye, self_score, score_own) + bo_ref[head]
                top = jnp.max(score_own, axis=1, keepdims=True)
                if full:
                    score_ext = nt(queries, key_ext) + be_ref[head]
                    top = jnp.maximum(top, jnp.max(score_ext, axis=1, keepdims=True))
                part_own = jnp.exp(score_own - top)
                total = jnp.sum(part_own, axis=1, keepdims=True)
                if full:
                    part_ext = jnp.exp(score_ext - top)
                    total = total + jnp.sum(part_ext, axis=1, keepdims=True)
                inverse = 1.0 / total
                weight_own = (part_own * inverse).astype(bf16)
                po_ref[0, stream, head] = weight_own
                out = nn(weight_own, vo_ref[0])
                if full:
                    weight_ext = (part_ext * inverse).astype(bf16)
                    pe_ref[0, stream, head] = weight_ext
                    out = out + nn(weight_ext, ve_ref[0])
                outs.append(out)
            a_ref[0, stream] = jnp.where(lane < HDIM, outs[0], outs[1]).astype(bf16)

    is_full = full_ref[slot] > 0

    @pl.when(is_full)
    def _():
        run(True)

    @pl.when(jnp.logical_not(is_full))
    def _():
        run(False)


def specs_of(rows, ext, pairs, slots):
    def far_slot(s, full):
        if slots != 2:
            return s
        return jnp.where(full[s] > 0, s, jnp.where(full[1 - s] > 0, 1 - s, 0))

    def far_pair(p, full):
        if slots != 2:
            return p
        return jnp.where(full[0] + full[1] > 0, p, 0)

    def near(at):
        return pl.BlockSpec((1, rows, LANES), lambda p, s, full: (s, 0, p + at))

    def far(at):
        return pl.BlockSpec(
            (1, ext, LANES), lambda p, s, full: (far_slot(s, full), 0, far_pair(p, full) + at)
        )

    def pair(at):
        return pl.BlockSpec((1, 2, rows, LANES), lambda p, s, full: (s, 0, 0, p + at))

    own_lanes = pl.BlockSpec((1, rows, LANES), lambda p, s, full: (s, 0, 0))
    far_lanes = pl.BlockSpec((1, ext, LANES), lambda p, s, full: (far_slot(s, full), 0, 0))
    query_lanes = pl.BlockSpec((1, 2, rows, LANES), lambda p, s, full: (s, 0, 0, 0))
    weight_own = pl.BlockSpec((1, 2, 2, rows, rows), lambda p, s, full: (s, 0, p, 0, 0))
    weight_far = pl.BlockSpec(
        (1, 2, 2, rows, ext), lambda p, s, full: (far_slot(s, full), 0, far_pair(p, full), 0, 0)
    )
    heads = [near(0), near(0), near(pairs), near(2 * pairs), far(0), far(pairs)]
    return heads, pair, own_lanes, far_lanes, query_lanes, weight_own, weight_far


def per_head(*shape):
    return pl.BlockSpec((2,) + shape, lambda p, s, full: (p,) + (0,) * len(shape))


def attend(full, blocks, lanes, tables, diagonals):
    qkv, query, far_kv = blocks
    slots, rows, width = query.shape
    ext = far_kv.shape[1]
    heads = width // HDIM
    query_lanes, own_lanes, ext_lanes, seg_rows = lanes
    specs, pair, own_l, far_l, query_l, w_own, w_far = specs_of(rows, ext, heads // 2, slots)
    return pl.pallas_call(
        attend_kernel,
        grid_spec=pltpu.PrefetchScalarGridSpec(
            num_scalar_prefetch=1,
            grid=(heads // 2, slots),
            in_specs=specs + [
                query_l, own_l, far_l, own_l,
                per_head(2 * LANES, 2 * LANES), per_head(2, LANES), per_head(2 * LANES, LANES),
                per_head(1, diagonals.shape[-1]),
            ],
            out_specs=[pair(0), w_own, w_far],
            scratch_shapes=[pltpu.VMEM((2, rows, rows), f32), pltpu.VMEM((2, rows, ext), f32)],
        ),
        out_shape=[
            jax.ShapeDtypeStruct((slots, 2, rows, width), bf16),
            jax.ShapeDtypeStruct((slots, 2, heads, rows, rows), bf16),
            jax.ShapeDtypeStruct((slots, 2, heads, rows, ext), bf16),
        ],
    )(full, qkv, query, qkv, qkv, far_kv, far_kv, query_lanes, own_lanes, ext_lanes, seg_rows,
      *tables, diagonals)


def attend_back_kernel(
    full_ref, qc_ref, qg_ref, ko_ref, vo_ref, ke_ref, ve_ref, kmo_ref, kme_ref, seg_ref,
    a_ref, da_ref, po_ref, pe_ref, emb_ref, cb_ref,
    dq_ref, dko_ref, dke_ref, small_ref, diag_ref,
    bo_ref, be_ref,
):
    slot = pl.program_id(1)
    rows = qc_ref.shape[1]
    ext = ke_ref.shape[1]
    lane = lane_of((rows, LANES))

    @pl.when(slot == 0)
    def _():
        bo_ref[...] = jnp.zeros_like(bo_ref)
        be_ref[...] = jnp.zeros_like(be_ref)
        small_ref[...] = jnp.zeros_like(small_ref)

    def keys_of(k_ref, km_ref, head):
        key_lane = lane_of(k_ref.shape[1:])
        return jnp.where(key_lane // HDIM == head, k_ref[0], km_ref[0])

    def run(full):
        parts = [(ko_ref, vo_ref, kmo_ref, po_ref, bo_ref, dko_ref)]
        if full:
            parts.append((ke_ref, ve_ref, kme_ref, pe_ref, be_ref, dke_ref))
        d_queries = [[None, None], [None, None]]
        for head in range(2):
            own = lane // HDIM == head
            base = HDIM * (1 - head)
            key_sets = [keys_of(k_ref, km_ref, head) for k_ref, _, km_ref, *_ in parts]
            d_keys = [0.0] * len(parts)
            d_values = [0.0] * len(parts)
            totals = [jnp.zeros((1, LANES), f32)] * 5
            for stream in range(2):
                queries = (qc_ref, qg_ref)[stream][0]
                flat = jnp.where(
                    own,
                    queries.astype(f32) * SCALE,
                    jnp.where(lane % HDIM == 4, 1.0, 0.0),
                ).astype(bf16)
                cot = jnp.where(own, da_ref[0, stream].astype(f32), 0.0)
                inner = jnp.sum(cot * a_ref[0, stream].astype(f32), axis=1, keepdims=True)
                cot = cot.astype(bf16)
                d_rows = 0.0
                for at, (k_ref, v_ref, km_ref, p_ref, b_ref, dk_ref) in enumerate(parts):
                    weights = p_ref[0, stream, head]
                    d_scores = weights.astype(f32) * (nt(cot, v_ref[0]) - inner)
                    b_ref[head] += d_scores
                    d_scores = d_scores.astype(bf16)
                    d_rows = d_rows + nn(d_scores, key_sets[at])
                    d_keys[at] = d_keys[at] + tn(flat, d_scores)
                    d_values[at] = d_values[at] + tn(cot, weights)
                every = d_rows[:, base : base + 1]
                ones = d_rows[:, base + 2 : base + 3]
                same = jnp.where(seg_ref[0] > 0, ones, every - ones)
                other = every - same
                d_queries[stream][head] = SCALE * (
                    d_rows + other * emb_ref[head, 0:1] + same * emb_ref[head, 1:2]
                )
                wide = queries.astype(f32)
                for row, member in enumerate((other * wide, same * wide, other, same, d_rows)):
                    totals[row] = totals[row] + jnp.sum(member, axis=0, keepdims=True)
            for row in range(5):
                small_ref[head, row : row + 1] += totals[row]
            for at, (k_ref, v_ref, km_ref, p_ref, b_ref, dk_ref) in enumerate(parts):
                column = d_keys[at][base + 4 : base + 5]
                mine = slice(HDIM * head, HDIM * head + HDIM)
                dk_ref[0, 0, mine] = (d_keys[at][mine] + cb_ref[head] * SCALE * column).astype(bf16)
                dk_ref[0, 1, mine] = d_values[at][mine].astype(bf16)
        for stream in range(2):
            dq_ref[0, stream] = jnp.where(lane < HDIM, d_queries[stream][0], d_queries[stream][1]).astype(bf16)

    is_full = full_ref[slot] > 0

    @pl.when(is_full)
    def _():
        run(True)

    @pl.when(jnp.logical_not(is_full))
    def _():
        run(False)
        dke_ref[...] = jnp.zeros_like(dke_ref)

    @pl.when(slot == pl.num_programs(1) - 1)
    def _():
        for head in range(2):
            start = 0
            for ref, at, width in ((bo_ref, 0, rows), (be_ref, 0, rows), (be_ref, rows, ext - rows)):
                length = width + rows
                block = jnp.concatenate([ref[head, :, at : at + width], jnp.zeros((rows, rows), f32)], axis=1)
                step = rows // 2
                while step >= 8:
                    block = block[:step] + pltpu.roll(block[step:], length - step, 1)
                    step //= 2
                while step >= 1:
                    block = block + pltpu.roll(pltpu.roll(block, length - step, 1), 8 - step, 0)
                    step //= 2
                diag_ref[head, :, start : start + length] = block[:1]
                start += length


def attend_back(full, blocks, lanes, attended, d_attended, at, weights, embed_rows, bias_columns, diag_length):
    qkv, query, far_kv = blocks
    slots, rows, width = query.shape
    ext = far_kv.shape[1]
    heads = width // HDIM
    pairs = heads // 2
    _, own_lanes, ext_lanes, seg_rows = lanes
    specs, pair, own_l, far_l, _, w_own, w_far = specs_of(rows, ext, pairs, slots)
    return pl.pallas_call(
        attend_back_kernel,
        grid_spec=pltpu.PrefetchScalarGridSpec(
            num_scalar_prefetch=1,
            grid=(pairs, slots),
            in_specs=specs + [
                own_l, far_l, own_l, pair(0), pair(at), w_own, w_far, per_head(2, LANES), per_head(HDIM, 1),
            ],
            out_specs=[
                pair(0),
                pl.BlockSpec((1, 2, LANES, rows), lambda p, s, full: (s, 0, p, 0)),
                pl.BlockSpec((1, 2, LANES, ext), lambda p, s, full: (s, 0, p, 0)),
                per_head(8, LANES),
                per_head(1, diag_length),
            ],
            scratch_shapes=[pltpu.VMEM((2, rows, rows), f32), pltpu.VMEM((2, rows, ext), f32)],
        ),
        out_shape=[
            jax.ShapeDtypeStruct((slots, 2, rows, width), bf16),
            jax.ShapeDtypeStruct((slots, 2, width, rows), bf16),
            jax.ShapeDtypeStruct((slots, 2, width, ext), bf16),
            jax.ShapeDtypeStruct((heads, 8, LANES), f32),
            jax.ShapeDtypeStruct((heads, 1, diag_length), f32),
        ],
    )(full, qkv, query, qkv, qkv, far_kv, far_kv, own_lanes, ext_lanes, seg_rows,
      attended, d_attended, weights[0], weights[1], embed_rows, bias_columns)


def swap(values_in, axis_name):
    size = lax.axis_size(axis_name)
    return lax.ppermute(values_in, axis_name, [(i, (i + 1) % size) for i in range(size)])


def ordered(bit, mine, other, axis):
    first = jnp.where(bit == 0, mine, other)
    second = jnp.where(bit == 0, other, mine)
    return jnp.concatenate([first, second], axis=axis)


def piece_of(values_in, at, count, axis=0):
    size = values_in.shape[axis] // count
    return lax.dynamic_slice_in_dim(values_in, at * size, size, axis)


def fetch_half(values_in, core, axis):
    piece = piece_of(values_in, core, 2, axis)
    near = swap(piece, "t")
    return near, swap(near, "c")


def add_low(first, second):
    return (first.astype(f32) + second.astype(f32)).astype(bf16)


def sum_over_groups(total):
    groups = lax.axis_size("o")
    pieces = total.reshape(groups, -1, total.shape[-1])
    arrived = lax.all_to_all(pieces, "o", 0, 0)
    mine = jnp.sum(arrived.astype(f32), axis=0).astype(bf16)
    whole = lax.all_to_all(jnp.broadcast_to(mine[None], arrived.shape), "o", 0, 0)
    return whole.reshape(total.shape), mine


def padded(values_in):
    rows = values_in.shape[-2]
    block = 32 * lax.axis_size("o")
    return jnp.pad(values_in, [(0, 0)] * (values_in.ndim - 2) + [(0, -rows % block), (0, 0)])


def after(values_in, *others):
    return lax.optimization_barrier((values_in,) + others)[0]


def norm_parts(values_in):
    centred = values_in - jnp.mean(values_in, axis=-1, keepdims=True)
    spread = jnp.mean(centred * centred, axis=-1, keepdims=True)
    return centred, lax.rsqrt(spread + epsilon)


def norm_back(cotangent, gain, centred, inverse):
    unit = centred * inverse
    scaled = cotangent * gain
    first = jnp.mean(scaled, axis=-1, keepdims=True)
    second = jnp.mean(scaled * unit, axis=-1, keepdims=True)
    return inverse * (scaled - first - unit * second), unit


def gelu_pair(values_in):
    rate = 0.7978845608028654
    square = values_in * values_in
    bent = jnp.tanh(rate * values_in * (1.0 + 0.044715 * square))
    half = 0.5 * (1.0 + bent)
    slope = half + 0.5 * values_in * (1.0 - bent * bent) * rate * (1.0 + 3 * 0.044715 * square)
    return values_in * half, slope


def dot_to(equation, left, right):
    return jnp.einsum(equation, left, right, preferred_element_type=f32)


def per_device(
    h_in, g_in, mem_in, d_h_out, d_g_out, w_query, w_key, w_value, w_out, content_bias, seg_bias,
    seg_embed, rel_table, norm1_gain, norm1_bias, w_in, b_in, w_ffo, b_ffo, norm2_gain, norm2_bias,
    bucket_len, doc_len, seg_ids, mem_seg, perm_rank,
):
    half = lax.axis_index("t")
    core = lax.axis_index("c")
    content, stream, memory = h_in[0], g_in[0], mem_in[0]
    slots, rows, width = content.shape
    mem_half = memory.shape[1]
    slot_rows = perm_rank.shape[2]
    mem_rows = mem_seg.shape[2]
    heads_width = w_query.shape[1]
    heads_half = heads_width // HDIM

    kv_rows = jnp.concatenate([content, memory], axis=1)
    other_rows = swap(kv_rows, "t")
    proj_own = jnp.concatenate([w_query, w_key, w_value], axis=1)
    proj_far = ordered(core, *fetch_half(after(proj_own, kv_rows), core, 0), 0)
    w_out_far = fetch_half(after(w_out, other_rows), core, 0)
    w_out_all = jnp.concatenate([w_out, ordered(core, *w_out_far, 0)], axis=0)
    table_half = jnp.concatenate(
        [content_bias, seg_bias, seg_embed[0], seg_embed[1], rel_table], axis=1
    )
    small_half = jnp.concatenate([table_half.reshape(-1), b_in])
    small_other = swap(small_half, "t")
    cut = table_half.size
    tables = jnp.concatenate([table_half, small_other[:cut].reshape(table_half.shape)], axis=0)
    content_all, seg_all = tables[:, :HDIM], tables[:, HDIM : 2 * HDIM]
    embed_all = jnp.stack([tables[:, 2 * HDIM : 3 * HDIM], tables[:, 3 * HDIM : 4 * HDIM]])
    rel_all = tables[:, 4 * HDIM :]
    ff_half = w_in.shape[1]
    w_in_near, w_in_far = fetch_half(after(w_in, other_rows), core, 1)
    w_in_all = jnp.concatenate([w_in, w_in_near, w_in_far], axis=1)
    w_ffo_near, w_ffo_far = fetch_half(after(w_ffo, w_out_far[0]), core, 0)
    w_ffo_all = jnp.concatenate([w_ffo, w_ffo_near, w_ffo_far], axis=0)
    bias_other = small_other[cut:]
    hidden_bias = jnp.concatenate(
        [b_in, piece_of(bias_other, core, 2), piece_of(bias_other, 1 - core, 2)]
    )

    full = (bucket_len[0] == slot_rows).astype(jnp.int32)
    query_lanes, key_lanes, mem_lanes = jax.vmap(mask_lanes)(
        bucket_len[0], doc_len[0], perm_rank[0], seg_ids[0], mem_seg[0]
    )
    start = half * rows
    far = slot_rows - rows - start

    def own_of(values_in, axis):
        return lax.dynamic_slice_in_dim(values_in, start, rows, axis)

    seg_rows = jnp.broadcast_to(
        own_of(seg_ids[0], 1).astype(f32)[:, :, None], (slots, rows, LANES)
    )
    lanes = (
        own_of(query_lanes, 2),
        own_of(key_lanes, 1),
        jnp.concatenate([lax.dynamic_slice_in_dim(key_lanes, far, rows, 1), mem_lanes], axis=1),
        seg_rows,
    )
    head_set = head_tables(content_all, seg_all, embed_all)
    buckets = diagonal_buckets(half, rows, mem_rows)
    hot = (buckets[None] == jnp.arange(NREL, dtype=jnp.int32)[:, None]).astype(f32)
    diagonals = jnp.dot(rel_all, hot, precision=highest)[:, None]

    def project(values_in, weight):
        return dot_to("sjd,de->sje", values_in, weight).astype(bf16)

    ext_rows = jnp.concatenate(
        [other_rows[:, :rows], ordered(half, memory, other_rows[:, rows:], 1)], axis=1
    )

    def blocks_of(weight):
        near = project(content, weight), project(stream, weight[:, :heads_width])
        return near + (project(ext_rows, weight[:, heads_width:]),)

    def part_of(values_in, at):
        return values_in[heads_half * at : heads_half * (at + 1)]

    heads_in = []
    forward = []
    for at, weight in enumerate((proj_own, proj_far)):
        heads_in.append(blocks_of(weight))
        forward.append(
            attend(
                full, heads_in[at], lanes, [part_of(table, at) for table in head_set],
                part_of(diagonals, at),
            )
        )

    flat_rows = slots * 2 * rows
    pair_flat = jnp.stack([content, stream], axis=1).reshape(flat_rows, width)
    attended = [member[0].reshape(flat_rows, heads_width) for member in forward]
    mid = (
        pair_flat.astype(f32)
        + dot_to("re,ed->rd", attended[0], w_out_all[:heads_width])
        + dot_to("re,ed->rd", attended[1], w_out_all[heads_width:])
    )
    centred1, inverse1 = norm_parts(mid)
    normed = centred1 * inverse1 * norm1_gain + norm1_bias
    normed_low = normed.astype(bf16)
    hidden = dot_to("rd,df->rf", normed_low, w_in_all) + hidden_bias
    active, slope = gelu_pair(hidden)
    active = active.astype(bf16)
    second = normed + dot_to("rf,fd->rd", active, w_ffo_all) + b_ffo
    centred2, inverse2 = norm_parts(second)
    outputs = (centred2 * inverse2 * norm2_gain + norm2_bias).astype(bf16).reshape(slots, 2, rows, width)

    cot = jnp.stack([d_h_out[0], d_g_out[0]], axis=1).reshape(flat_rows, width).astype(f32)
    d_second, unit2 = norm_back(cot, norm2_gain, centred2, inverse2)
    d_norm2_gain = jnp.sum(cot * unit2, axis=0)
    d_norm2_bias = jnp.sum(cot, axis=0)
    d_ffn = d_second.astype(bf16)
    d_b_ffo = jnp.sum(d_ffn.astype(f32), axis=0)
    ff_quarter = ff_half // 2
    far_start = ff_half + ff_quarter

    chip_totals = []

    def chip_parts(own_half, near, far_piece, axis):
        sent = jnp.concatenate([piece_of(own_half, 1 - core, 2, axis), far_piece], axis=axis)
        kept = jnp.concatenate([piece_of(own_half, core, 2, axis), near], axis=axis)
        total = add_low(kept, swap(sent, "c"))
        chip_totals.append(total)
        size = near.shape[axis]
        mine = lax.slice_in_dim(total, 0, size, axis=axis)
        away = lax.slice_in_dim(total, size, 2 * size, axis=axis)
        arrived = swap(away, "t")
        return mine, arrived

    d_w_ffo = dot_to("rf,rd->fd", active, d_ffn).astype(bf16)
    ffo_parts = chip_parts(d_w_ffo[:ff_half], d_w_ffo[ff_half:far_start], d_w_ffo[far_start:], 0)
    d_hidden = (dot_to("rd,fd->rf", after(d_ffn, d_w_ffo), w_ffo_all) * slope).astype(bf16)
    d_b_in = jnp.sum(d_hidden.astype(f32), axis=0)
    d_w_in = dot_to("rd,rf->df", normed_low, d_hidden).astype(bf16)
    in_parts = chip_parts(
        d_w_in[:, :ff_half], d_w_in[:, ff_half:far_start], d_w_in[:, far_start:], 1
    )
    d_normed = d_second + dot_to("rf,df->rd", after(d_hidden, d_w_in, chip_totals[0]), w_in_all)
    d_mid, unit1 = norm_back(d_normed, norm1_gain, centred1, inverse1)
    d_norm1_gain = jnp.sum(d_normed * unit1, axis=0)
    d_norm1_bias = jnp.sum(d_normed, axis=0)
    d_attn = d_mid.astype(bf16)
    d_attended = dot_to("rd,ed->re", d_attn, w_out_all).astype(bf16).reshape(slots, 2, rows, width)

    shared = jnp.concatenate([d_norm1_gain, d_norm1_bias, d_norm2_gain, d_norm2_bias, d_b_ffo])
    shared = shared.reshape(-1, width)
    bias_far = ordered(core, d_b_in[ff_half:far_start], d_b_in[far_start:], 0)
    own_rest, far_rest = [
        padded(jnp.concatenate(
            [dot_to("re,rd->ed", attended[at], d_attn).astype(bf16), shared.astype(bf16),
             bias.reshape(-1, width).astype(bf16)]
        ))
        for at, bias in enumerate((d_b_in[:ff_half], bias_far))
    ]
    rest_parts = chip_parts(
        own_rest, piece_of(far_rest, core, 2), piece_of(far_rest, 1 - core, 2), 0
    )
    ffn_chip = jnp.concatenate(
        [add_low(*parts) for parts in (ffo_parts, in_parts, rest_parts)], axis=0
    )
    ffn_sum = lax.psum(ffn_chip, "o")
    embed_rows = jnp.transpose(embed_all, (1, 0, 2))
    embed_rows = jnp.concatenate([embed_rows, embed_rows], axis=-1)
    odd = (jnp.arange(heads_half) % 2)[:, None, None]
    backward = {}
    small_size = heads_half * (4 * HDIM + NREL)
    gate = after(d_attended, *chip_totals)
    for at in (1, 0):
        d_query, d_near, d_far, small, diag = attend_back(
            full, heads_in[at], lanes, forward[at][0], gate, at * (heads_half // 2), forward[at][1:],
            part_of(embed_rows, at), part_of(content_all, at)[:, :, None], diagonals.shape[-1],
        )
        d_flat = d_query.reshape(flat_rows, heads_width)
        d_near = d_near.reshape(slots, 2 * heads_width, rows)
        d_far = d_far.reshape(slots, 2 * heads_width, ext_rows.shape[1])
        backward[at] = d_flat, d_near, d_far
        d_wq = dot_to("re,rd->ed", d_flat, pair_flat).astype(bf16)
        d_wkv = (
            dot_to("sej,sjd->ed", d_near, content) + dot_to("sej,sjd->ed", d_far, ext_rows)
        ).astype(bf16)
        d_rel = jnp.einsum("hl,rl->hr", diag[:, 0], hot, precision=highest) * SCALE
        small = jnp.where(odd == 0, small[:, :, :HDIM], small[:, :, HDIM:]) * SCALE
        seg_part, embed_part = part_of(seg_all, at), [part_of(member, at) for member in embed_all]
        head_small = jnp.concatenate(
            [
                small[:, 4],
                small[:, 2] * embed_part[0] + small[:, 3] * embed_part[1],
                small[:, 0] + small[:, 2] * seg_part,
                small[:, 1] + small[:, 3] * seg_part,
                d_rel,
            ],
            axis=1,
        ).reshape(-1)
        head_small = jnp.pad(head_small, (0, -small_size % width)).reshape(-1, width)
        block = padded(jnp.concatenate([d_wq, d_wkv, head_small.astype(bf16)]))
        chip = add_low(piece_of(block, core, 2), swap(piece_of(block, 1 - core, 2), "c"))
        if at == 1:
            arrived = swap(chip, "t")
            gate = after(d_attended, chip)
        else:
            proj_sum, proj_first = sum_over_groups(add_low(chip, arrived))
    proj_sums = ordered(core, proj_sum, swap(proj_sum, "c"), 0)

    weights_back = [weight[:, heads_width:] for weight in (proj_own, proj_far)]

    def back_keys(place):
        return dot_to("sej,de->sjd", backward[1][place], weights_back[1]) + dot_to(
            "sej,de->sjd", backward[0][place], weights_back[0]
        )

    d_ext = back_keys(2).astype(bf16)
    mem_mine = jnp.where(half == 0, d_ext[:, rows : rows + mem_half], d_ext[:, rows + mem_half :])
    mem_away = jnp.where(half == 0, d_ext[:, rows + mem_half :], d_ext[:, rows : rows + mem_half])
    arrived_rows = swap(jnp.concatenate([d_ext[:, :rows], mem_away], axis=1), "t").astype(f32)
    d_pair = (
        d_mid
        + dot_to("re,de->rd", backward[1][0], proj_far[:, :heads_width])
        + dot_to("re,de->rd", backward[0][0], proj_own[:, :heads_width])
    ).reshape(slots, 2, rows, width)
    d_content = d_pair[:, 0] + back_keys(1) + arrived_rows[:, :rows]
    d_memory = mem_mine.astype(f32) + arrived_rows[:, rows:]

    ffn_sum = after(ffn_sum, arrived_rows, proj_first)
    ffn_other = swap(ffn_sum, "c")
    in_end = ff_quarter + width
    ffo_sums = ordered(core, ffn_sum[:ff_quarter], ffn_other[:ff_quarter], 0)
    in_sums = ordered(core, ffn_sum[ff_quarter:in_end], ffn_other[ff_quarter:in_end], 1)
    rest_sums = ordered(core, ffn_sum[in_end:], ffn_other[in_end:], 0)

    vectors = rest_sums[heads_width : heads_width + 5].astype(f32)
    sum_b_in = rest_sums[heads_width + 5 :][: ff_half // width].astype(f32).reshape(-1)
    per_head_sums = proj_sums[3 * heads_width :].reshape(-1)[:small_size].astype(f32)
    per_head_sums = per_head_sums.reshape(heads_half, 4 * HDIM + NREL)
    d_small = [per_head_sums[:, HDIM * c : HDIM * (c + 1)] for c in range(4)]
    blocks = [proj_sums[heads_width * c : heads_width * (c + 1)].astype(f32).T for c in range(3)]
    return (
        outputs[:, 0][None],
        outputs[:, 1][None],
        d_content.astype(bf16)[None],
        d_pair[:, 1].astype(bf16)[None],
        d_memory.astype(bf16)[None],
        blocks[0],
        blocks[1],
        blocks[2],
        rest_sums[:heads_width].astype(f32),
        d_small[0],
        d_small[1],
        jnp.stack([d_small[2], d_small[3]]),
        per_head_sums[:, 4 * HDIM :],
        vectors[0],
        vectors[1],
        in_sums.astype(f32),
        sum_b_in,
        ffo_sums.astype(f32),
        vectors[4],
        vectors[2],
        vectors[3],
    )


def solution(mesh):
    groups = mesh.shape["dp"] // 2
    split = Mesh(mesh.devices.reshape(groups, 2, -1), ("o", "c", "t"))
    dp = ("o", "c")
    rows = P(dp, None, "t", None)
    columns = P(None, "t")
    lead = P("t", None)
    group = P(dp, None, None)
    return jax.shard_map(
        per_device,
        mesh=split,
        in_specs=(
            rows, rows, rows, rows, rows, columns, columns, columns, lead, lead, lead,
            P(None, "t", None), lead, P(), P(), columns, P("t"), lead, P(), P(), P(),
            P(dp, None), group, group, group, group,
        ),
        out_specs=(
            rows, rows, rows, rows, rows, columns, columns, columns, lead, lead, lead,
            P(None, "t", None), lead, P(), P(), columns, P("t"), lead, P(), P(), P(),
        ),
        check_vma=False,
    )
```
